32 devices in a mesh: sec: 4 (over y, x), gx: 8 (over z, core).
Axes of the slice: x: 2, y: 2, z: 4, core: 2. Of those that a mesh axis runs over, the one named last changes fastest.
Arguments:
- pressure_start: float32 [16, 128, 1024], P('sec', 'gx'), may hold values from -8 to 8
- soil_type: int32 [16, 128, 1024], P('sec', 'gx'), may hold values from 0 to 11
- saturated_conductivity: float32 [12], replicated, may hold values from 0.2 to 5
- storage_coefficient: float32 [12], replicated, may hold values from 0.1 to 1
- rainfall: float32 [3, 128, 1024], P(None, 'gx'), may hold values from 0 to 2
Outputs:
- pressure: float32 [16, 128, 1024], P('sec', 'gx')
- inflow: float32 [4, 3, 128, 1024], P('sec', None, 'gx')
The draws below stay inside these ranges and needn't reach their ends.
All inputs are finite; a program needn't handle non-finite values.
Results may differ from the reference program's by a relative error of at most 0.0001.
Values sent between devices are 32-bit elements; how exact they have to be, the bound alone decides.
A program may use at most 64 MiB of HBM per device.

```python
import math
import jax
import jax.numpy as jnp

LZ = 4
STEPS = 3
ITERS = 4
SOILS = 12
NZ = 16
NX = 128
NY = 1024
N_SEC = 4


def touch_ends(array, stream_key, low, high):
    longest = array.shape.index(max(array.shape))
    spots = []
    for shift in (0, 1):
        where = [jax.random.randint(jax.random.fold_in(stream_key, axis), (), 0, length) for axis, length in enumerate(array.shape)]
        where[longest] = (where[longest] + shift) % array.shape[longest]
        spots.append(tuple(where))
    return array.at[spots[0]].set(low).at[spots[1]].set(high)


def levels(rng, extent, split, smallest, largest):
    factor_of = 1.0
    for axis_at, parts in split:
        steps = jax.random.uniform(jax.random.fold_in(jax.random.fold_in(rng, 6), axis_at), (parts,), jnp.float32, smallest / len(split), largest / len(split))
        factor_of = factor_of * jnp.repeat(jnp.exp(steps), extent[axis_at] // parts).reshape((-1,) + (1,) * (len(extent) - 1 - axis_at))
    return factor_of


def bell_draw(stream_key, dims, deviation, bound, split=(), held_as=jnp.bfloat16):
    values = jax.random.normal(stream_key, dims, jnp.float32) * deviation
    if len(split) > 0:
        values = levels(stream_key, dims, split, -0.22, 0.18) * values
    return jnp.clip(values, min=-bound, max=bound).astype(held_as)


def setup_inputs(seed: int = 0) -> dict:
    key_list = jax.random.split(jax.random.key(seed), 6)
    return {
        "pressure_start": bell_draw(key_list[0], (NZ, NX, NY), 1.5, 8.0, ((0, 4), (1, 8)), jnp.float32),
        "soil_type": touch_ends(jax.random.randint(key_list[1], (NZ, NX, NY), 0, SOILS), jax.random.fold_in(key_list[1], 1), 0, SOILS - 1).astype(jnp.int32),
        "saturated_conductivity": jnp.clip(jnp.exp(jax.random.uniform(key_list[2], (SOILS,), jnp.float32, math.log(0.2), math.log(5.0))), 0.2, 5.0),
        "storage_coefficient": jnp.clip(jnp.exp(jax.random.uniform(key_list[3], (SOILS,), jnp.float32, math.log(0.1), math.log(1.0))), 0.1, 1.0),
        "rainfall": jnp.clip(2.0 * jax.random.uniform(key_list[4], (STEPS, NX, NY), jnp.float32) ** levels(key_list[4], (STEPS, NX, NY), ((1, 8),), -0.2, 0.2), 0.0, 2.0),
    }


def harmonic(cond, other):
    return 2.0 * cond * other / (cond + other)


def neighbours(padded):
    return [padded[:-2, 1:-1, 1:-1], padded[2:, 1:-1, 1:-1], padded[1:-1, :-2, 1:-1],
            padded[1:-1, 2:, 1:-1], padded[1:-1, 1:-1, :-2], padded[1:-1, 1:-1, 2:]]


def operate(field, faces, capacity):
    result = capacity * field
    for face, other in zip(faces, neighbours(jnp.pad(field, 1))):
        result = result + face * (field - other)
    return result


def reference(pressure_start, soil_type, saturated_conductivity, storage_coefficient, rainfall):
    cond_table = saturated_conductivity[soil_type]
    store_table = storage_coefficient[soil_type]
    head = pressure_start
    flows = []
    for step in range(STEPS):
        saturation = jax.nn.sigmoid(head)
        conductivity = cond_table * (0.05 + saturation * saturation)
        capacity = store_table * (0.1 + saturation * (1.0 - saturation))
        faces = [harmonic(conductivity, other) for other in neighbours(jnp.pad(conductivity, 1))]
        water = jnp.sum(saturation.reshape(N_SEC, LZ, NX, NY), axis=1)
        bottom = conductivity.reshape(N_SEC, LZ, NX, NY)[:, LZ - 1]
        depth = jnp.float32(LZ)
        below = jnp.zeros((NX, NY), jnp.float32)
        slopes = [None] * N_SEC
        for section in reversed(range(N_SEC)):
            slopes[section] = (water[section] / depth) * (0.5 + 0.5 * below / (below + depth))
            below = below + water[section]
        prefix_a = jnp.ones((NX, NY), jnp.float32)
        prefix_b = jnp.zeros((NX, NY), jnp.float32)
        inflows = []
        sources = []
        for section in range(N_SEC):
            entering = prefix_a * rainfall[step] + prefix_b
            offset = 0.5 * bottom[section]
            leaving = slopes[section] * entering + offset
            inflows.append(entering)
            local = jnp.zeros((LZ, NX, NY), jnp.float32).at[0].add(entering).at[LZ - 1].add(-leaving)
            sources.append(local)
            prefix_b = slopes[section] * prefix_b + offset
            prefix_a = slopes[section] * prefix_a
        flows.append(jnp.stack(inflows))
        source = jnp.concatenate(sources, axis=0)
        gravity = faces[0] - faces[1]
        rhs = capacity * head + gravity + source
        diagonal = capacity
        for face in faces:
            diagonal = diagonal + face
        iterate = head
        residual = rhs - operate(iterate, faces, capacity)
        precond = residual / diagonal
        direction = precond
        product = jnp.sum(residual * precond)
        for turn in range(ITERS):
            image = operate(direction, faces, capacity)
            alpha = product / jnp.sum(direction * image)
            iterate = iterate + alpha * direction
            residual = residual - alpha * image
            if turn + 1 < ITERS:
                precond = residual / diagonal
                renewed = jnp.sum(residual * precond)
                direction = precond + (renewed / product) * direction
                product = renewed
        head = iterate
    return head, jnp.stack(flows, axis=1)
```

```python
import functools

import jax
import jax.numpy as jnp
from jax import lax
from jax.experimental import pallas as pl
from jax.experimental.pallas import tpu as pltpu
from jax.sharding import PartitionSpec as P


MESH = pl.DeviceIdType.MESH
RIM = 8
LANES = 128
ITERS = 4


def place_of(s):
    return s + s // 2 - 2 * (s // 3)


def coefficients(g, h):
    nu = [g[0], h[0]]
    for k in range(1, ITERS):
        nu.append(2.0 * g[k] - nu[0])
        nu.append(4.0 * h[k] - 2.0 * nu[1] - nu[2 * k - 1])

    def gram(i, j):
        return 0.5 * (nu[i + j] + nu[abs(i - j)])

    def gram_a(i, j):
        shifted = gram(i, 1) if j == 0 else 0.5 * (gram(i, j + 1) + gram(i, j - 1))
        return gram(i, j) - shifted

    G = [[gram(i, j) for j in range(ITERS)] for i in range(ITERS)]
    H = [[gram_a(max(i, j), min(i, j)) for j in range(ITERS)] for i in range(ITERS)]
    zero = jnp.zeros_like(g[0])

    def form(matrix, v, top):
        total = zero
        for i in range(top + 1):
            row = matrix[i][i] * v[i]
            for j in range(i):
                row = row + 2.0 * matrix[i][j] * v[j]
            total = total + row * v[i]
        return total

    z = [zero + 1.0] + [zero] * (ITERS - 1)
    p = list(z)
    x = [zero] * ITERS
    rz = nu[0]
    for k in range(ITERS):
        curve = form(H, p, k)
        alpha = jnp.where(curve > 0.0, rz / jnp.where(curve > 0.0, curve, 1.0), 0.0)
        x = [a + alpha * b for a, b in zip(x, p)]
        if k + 1 < ITERS:
            image = list(p)
            for i in range(k + 1):
                if i == 0:
                    image[1] = image[1] - p[0]
                else:
                    image[i + 1] = image[i + 1] - 0.5 * p[i]
                    image[i - 1] = image[i - 1] - 0.5 * p[i]
            z = [a - alpha * b for a, b in zip(z, image)]
            new = jnp.maximum(form(G, z, k + 1), 0.0)
            beta = jnp.where(rz > 0.0, new / jnp.where(rz > 0.0, rz, 1.0), 0.0)
            p = [a + beta * b for a, b in zip(z, p)]
            rz = new
    return x


def kernel(
    n_sec, n_gx, steps, kinds,
    start_ref, soil_ref, cond_ref, store_ref, rain_ref,
    out_ref, flow_ref,
    kind_mine, head, kind, store, cond, cap, face_l, face_r, face_c, diag, dinv, t0, t1, t2, t3,
    water, enter, leave, rainx, flows, pack_out, pack_in, stat_a, stat_b,
    own_sem, swap_send, swap_recv, col_send, col_recv, row_send, row_recv,
    a_send, a_recv, b_send, b_recv, back_send, back_recv,
):
    f32 = jnp.float32
    layers, rows, wide = start_ref.shape
    cols = wide // n_sec
    total = layers * n_sec
    sec, gx = lax.axis_index("sec"), lax.axis_index("gx")
    here = place_of(sec)
    ext_r, ext_c = rows + 2 * RIM, cols + LANES
    own = (slice(0, rows), slice(0, cols))

    def at(place):
        return pl.ds(pl.multiple_of(place * cols, LANES), cols)

    def layers_of(s):
        return pl.ds(1 + s * layers, layers)

    plane = jnp.zeros((ext_r, ext_c), f32)
    for ref in (head, kind, cond, t0, t1, t2, t3, face_l):
        ref[0] = plane
        ref[total + 1] = plane

    def clear(l, carry):
        for ref in (head, kind):
            ref[l, rows:, :] = jnp.zeros((2 * RIM, ext_c), f32)
        return carry

    lax.fori_loop(1, total + 1, clear, 0)
    for c in range(steps):
        rainx[c] = plane
    pack_in[...] = jnp.zeros_like(pack_in)
    kind_mine[...] = soil_ref[...].astype(f32) + 1.0

    sec_peers = [lax.rem(sec + k, n_sec) for k in range(1, n_sec)]
    gx_peers = [lax.rem(gx + k, n_gx) for k in range(1, n_gx)]
    barrier = pltpu.get_barrier_semaphore()
    for peer in sec_peers:
        pl.semaphore_signal(barrier, inc=1, device_id={"sec": peer}, device_id_type=MESH)
    for peer in gx_peers:
        pl.semaphore_signal(barrier, inc=1, device_id={"gx": peer}, device_id_type=MESH)

    lane = lax.broadcasted_iota(jnp.int32, (rows, LANES), 1)
    after = pl.multiple_of(lax.rem(here + 1, n_sec) * cols, LANES)
    before = pl.multiple_of(lax.rem(here + n_sec - 1, n_sec) * cols + cols - LANES, LANES)
    for c in range(steps):
        rainx[c, 0:rows, 0:cols] = rain_ref[c, :, at(here)]
        rainx[c, 0:rows, cols:] = jnp.where(
            lane < LANES // 2, rain_ref[c, :, pl.ds(after, LANES)], rain_ref[c, :, pl.ds(before, LANES)]
        )
    pl.semaphore_wait(barrier, n_sec + n_gx - 2)

    moves = []
    for f, (src, dst) in enumerate(((start_ref, head), (kind_mine, kind))):
        copy = pltpu.make_async_copy(
            src.at[:, :, at(here)], dst.at[layers_of(sec), 0:rows, 0:cols], own_sem.at[f]
        )
        copy.start()
        moves.append(copy)
        for k, peer in enumerate(sec_peers):
            copy = pltpu.make_async_remote_copy(
                src_ref=src.at[:, :, at(place_of(peer))],
                dst_ref=dst.at[layers_of(sec), 0:rows, 0:cols],
                send_sem=swap_send.at[f, k],
                recv_sem=swap_recv.at[f, k],
                device_id={"sec": peer},
                device_id_type=MESH,
            )
            copy.start()
            moves.append(copy)
    for copy in moves:
        copy.wait()

    def packed(field, low):
        outs = jnp.zeros((rows, LANES), f32)
        for l in range(total):
            if low:
                tile = field[1 + l, 0:rows, 0:LANES]
                shift = RIM * l
            else:
                tile = field[1 + l, 0:rows, cols - LANES:cols]
                shift = (RIM * l + RIM) % LANES
            moved = pltpu.roll(tile, shift, 1) if shift else tile
            outs = jnp.where(lane // RIM == l, moved, outs)
        return outs

    def send_cols(slot, field):
        pack_out[slot, 0] = packed(field, True)
        pack_out[slot, 1] = packed(field, False)
        for d in (0, 1):
            @pl.when(here > 0 if d == 0 else here < n_sec - 1)
            def _(d=d):
                col_copy(slot, d).start()

    def col_copy(slot, d):
        return pltpu.make_async_remote_copy(
            src_ref=pack_out.at[slot, d],
            dst_ref=pack_in.at[slot, d],
            send_sem=col_send.at[slot, d],
            recv_sem=col_recv.at[slot, d],
            device_id={"sec": place_of(lax.rem(here + n_sec - 1, n_sec) if d == 0 else lax.rem(here + 1, n_sec))},
            device_id_type=MESH,
        )

    def take_cols(slot, field):
        @pl.when(here > 0)
        def _():
            col_copy(slot, 0).wait_send()
            col_copy(slot, 1).wait_recv()

        @pl.when(here < n_sec - 1)
        def _():
            col_copy(slot, 1).wait_send()
            col_copy(slot, 0).wait_recv()

        right, left = pack_in[slot, 0], pack_in[slot, 1]
        for l in range(total):
            a, b = (-RIM * l) % LANES, (LANES - RIM - RIM * l) % LANES
            ra = pltpu.roll(right, a, 1) if a else right
            rb = pltpu.roll(left, b, 1) if b else left
            field[1 + l, 0:rows, cols:] = jnp.where(lane < RIM, ra, jnp.where(lane >= LANES - RIM, rb, 0.0))

    def row_copy(slot, field, first, count, d):
        src = pl.ds(0, RIM) if d == 0 else pl.ds(rows - RIM, RIM)
        dst = pl.ds(rows, RIM) if d == 0 else pl.ds(rows + RIM, RIM)
        return pltpu.make_async_remote_copy(
            src_ref=field.at[pl.ds(first, count), src, :],
            dst_ref=field.at[pl.ds(first, count), dst, :],
            send_sem=row_send.at[slot, d],
            recv_sem=row_recv.at[slot, d],
            device_id={"gx": lax.rem(gx + n_gx - 1, n_gx) if d == 0 else lax.rem(gx + 1, n_gx)},
            device_id_type=MESH,
        )

    def send_rows(*what):
        for d in (0, 1):
            @pl.when(gx > 0 if d == 0 else gx < n_gx - 1)
            def _(d=d):
                row_copy(*what, d).start()

    def take_rows(*what):
        @pl.when(gx > 0)
        def _():
            row_copy(*what, 0).wait_send()
            row_copy(*what, 1).wait_recv()

        @pl.when(gx < n_gx - 1)
        def _():
            row_copy(*what, 1).wait_send()
            row_copy(*what, 0).wait_recv()

    def shift(v, by, axis):
        return pltpu.roll(v, by % v.shape[axis], axis)

    def harmonic(a, b):
        return 2.0 * a * b / jnp.maximum(a + b, 1e-30)

    def folded(v):
        out = None
        for i in range(0, rows, RIM):
            for j in range(0, cols, LANES):
                part = v[i:i + RIM, j:j + LANES]
                out = part if out is None else out + part
        return out

    none = jnp.zeros((RIM, LANES), f32)
    basis = (t0, t1, t2, t3)

    for c in range(steps):
        send_cols(c, head)
        if c == 0:
            send_cols(steps, kind)
            send_rows(steps + 1, rainx, 0, steps)
        take_cols(c, head)
        send_rows(c, head, 1, total)
        if c == 0:
            take_cols(steps, kind)
            send_rows(steps, kind, 1, total)
            take_rows(steps + 1, rainx, 0, steps)
            take_rows(steps, kind, 1, total)

            def look(l, carry):
                here_kind = kind[l]
                a = jnp.zeros((ext_r, ext_c), f32)
                b = jnp.zeros((ext_r, ext_c), f32)
                for k in range(kinds):
                    same = here_kind == jnp.float32(k + 1)
                    a = jnp.where(same, cond_ref[k], a)
                    b = jnp.where(same, store_ref[k], b)
                kind[l] = a
                store[l] = b
                return carry

            lax.fori_loop(1, total + 1, look, 0)
        take_rows(c, head, 1, total)

        def soil(s, carry):
            amount = jnp.zeros((ext_r, ext_c), f32)
            for j in range(layers):
                l = 1 + s * layers + j
                sat = jax.nn.sigmoid(head[l])
                cond[l] = kind[l] * (0.05 + sat * sat)
                cap[l] = store[l] * (0.1 + sat * (1.0 - sat))
                amount = amount + sat
            water[s] = amount
            return carry

        lax.fori_loop(0, n_sec, soil, 0)

        depth = jnp.float32(layers)
        below = jnp.zeros((ext_r, ext_c), f32)
        for s in reversed(range(n_sec)):
            amount = water[s]
            water[s] = amount / depth * (0.5 + 0.5 * below / (below + depth))
            below = below + amount
        entering = rainx[c]
        for s in range(n_sec):
            enter[s] = entering
            flows[s, c] = entering[own]
            entering = water[s] * entering + 0.5 * cond[(s + 1) * layers]
            leave[s] = entering

        def faces(l, carry):
            k = cond[l]
            face_l[l] = harmonic(k, cond[l + 1])
            face_r[l] = harmonic(k, shift(k, -1, 0))
            face_c[l] = harmonic(k, shift(k, -1, 1))
            return carry

        lax.fori_loop(1, total + 1, faces, 0)

        def first(s, acc):
            for j in range(layers):
                l = 1 + s * layers + j
                up, down = face_l[l - 1], face_l[l]
                fr, fc = face_r[l], face_c[l]
                v = head[l]
                whole = cap[l] + up + down + fr + shift(fr, 1, 0) + fc + shift(fc, 1, 1)
                flux_r = fr * (shift(v, -1, 0) - v)
                flux_c = fc * (shift(v, -1, 1) - v)
                res = up - down + up * (head[l - 1] - v) + down * (head[l + 1] - v)
                res = res + flux_r - shift(flux_r, 1, 0) + flux_c - shift(flux_c, 1, 1)
                if j == 0:
                    res = res + enter[s]
                if j == layers - 1:
                    res = res - leave[s]
                inverse = jnp.where(whole > 0.0, 1.0 / jnp.maximum(whole, 1e-30), 0.0)
                z = res * inverse
                diag[l] = whole
                dinv[l] = inverse
                t0[l] = z
                acc = acc + folded(res * z)
            return acc

        g = [lax.fori_loop(0, n_sec, first, none)]
        h = []
        for k in range(ITERS):
            def apply(l, acc, k=k):
                t = basis[k]
                fr, fc = face_r[l], face_c[l]
                v = t[l]
                near = face_l[l - 1] * t[l - 1] + face_l[l] * t[l + 1]
                near = near + fr * shift(v, -1, 0) + shift(fr * v, 1, 0)
                near = near + fc * shift(v, -1, 1) + shift(fc * v, 1, 1)
                ah = acc[0] + folded(v * near)
                ag = acc[1]
                if k + 1 < ITERS:
                    new = dinv[l] * near
                    if k > 0:
                        new = 2.0 * new - basis[k - 1][l]
                    basis[k + 1][l] = new
                    ag = ag + folded(diag[l] * new * new)
                return (ah, ag)

            ah, ag = lax.fori_loop(1, total + 1, apply, (none, none))
            h.append(ah)
            if k + 1 < ITERS:
                g.append(ag)

        flat = [jnp.sum(v, axis=0, keepdims=True) for v in g + h]
        stat_a[c, sec] = jnp.concatenate(flat, axis=0)
        sends = []
        for k, peer in enumerate(sec_peers):
            copy = pltpu.make_async_remote_copy(
                src_ref=stat_a.at[c, sec],
                dst_ref=stat_a.at[c, sec],
                send_sem=a_send.at[c, k],
                recv_sem=a_recv.at[c, k],
                device_id={"sec": peer},
                device_id_type=MESH,
            )
            copy.start()
            sends.append(copy)
        for copy in sends:
            copy.wait()
        summed = stat_a[c, 0]
        for k in range(1, n_sec):
            summed = summed + stat_a[c, k]
        stat_b[c, gx] = summed
        sends = []
        for k, peer in enumerate(gx_peers):
            copy = pltpu.make_async_remote_copy(
                src_ref=stat_b.at[c, gx],
                dst_ref=stat_b.at[c, gx],
                send_sem=b_send.at[c, k],
                recv_sem=b_recv.at[c, k],
                device_id={"gx": peer},
                device_id_type=MESH,
            )
            copy.start()
            sends.append(copy)
        for copy in sends:
            copy.wait()
        summed = stat_b[c, 0]
        for k in range(1, n_gx):
            summed = summed + stat_b[c, k]
        sums = jnp.sum(summed, axis=1, keepdims=True)
        parts = [sums[k:k + 1] for k in range(2 * ITERS)]
        x = coefficients(parts[:ITERS], parts[ITERS:])
        x = [jnp.broadcast_to(v, (rows, cols)) for v in x]

        def update(l, carry):
            v = head[l, 0:rows, 0:cols]
            for k in range(ITERS):
                v = v + x[k] * basis[k][l, 0:rows, 0:cols]
            head[l, 0:rows, 0:cols] = v
            return carry

        lax.fori_loop(1, total + 1, update, 0)

    moves = []
    for f in range(2):
        def src(s):
            return head.at[layers_of(s), 0:rows, 0:cols] if f == 0 else flows.at[s]

        dst = out_ref.at[:, :, at(here)] if f == 0 else flow_ref.at[0, :, :, at(here)]
        copy = pltpu.make_async_copy(src(sec), dst, own_sem.at[2 + f])
        copy.start()
        moves.append(copy)
        for k, peer in enumerate(sec_peers):
            copy = pltpu.make_async_remote_copy(
                src_ref=src(peer),
                dst_ref=dst,
                send_sem=back_send.at[f, k],
                recv_sem=back_recv.at[f, k],
                device_id={"sec": peer},
                device_id_type=MESH,
            )
            copy.start()
            moves.append(copy)
    for copy in moves:
        copy.wait()


def body(n_sec, n_gx, start, soil, conductivity, storage, rain):
    layers, rows, wide = start.shape
    steps = rain.shape[0]
    cols = wide // n_sec
    total = layers * n_sec
    assert total * RIM <= LANES and cols % LANES == 0 and rows % RIM == 0 and n_sec == 4
    ext = (rows + 2 * RIM, cols + LANES)
    f32 = jnp.float32
    field = pltpu.VMEM((total + 2,) + ext, f32)
    per_sec = pltpu.VMEM((n_sec,) + ext, f32)
    dma = pltpu.SemaphoreType.DMA
    vmem = pl.BlockSpec(memory_space=pltpu.VMEM)
    smem = pl.BlockSpec(memory_space=pltpu.SMEM)
    return tuple(pl.pallas_call(
        functools.partial(kernel, n_sec, n_gx, steps, conductivity.shape[0]),
        out_shape=(
            jax.ShapeDtypeStruct(start.shape, f32),
            jax.ShapeDtypeStruct((1, steps, rows, wide), f32),
        ),
        in_specs=[vmem, vmem, smem, smem, vmem],
        out_specs=(vmem, vmem),
        scratch_shapes=[pltpu.VMEM(start.shape, f32)]
        + [field] * 14
        + [per_sec] * 3
        + [
            pltpu.VMEM((steps,) + ext, f32),
            pltpu.VMEM((n_sec, steps, rows, cols), f32),
            pltpu.VMEM((steps + 1, 2, rows, LANES), f32),
            pltpu.VMEM((steps + 1, 2, rows, LANES), f32),
            pltpu.VMEM((steps, n_sec, 2 * ITERS, LANES), f32),
            pltpu.VMEM((steps, n_gx, 2 * ITERS, LANES), f32),
            dma((4,)),
            dma((2, n_sec - 1)),
            dma((2, n_sec - 1)),
            dma((steps + 1, 2)),
            dma((steps + 1, 2)),
            dma((steps + 2, 2)),
            dma((steps + 2, 2)),
            dma((steps, n_sec - 1)),
            dma((steps, n_sec - 1)),
            dma((steps, n_gx - 1)),
            dma((steps, n_gx - 1)),
            dma((2, n_sec - 1)),
            dma((2, n_sec - 1)),
        ],
        compiler_params=pltpu.CompilerParams(collective_id=0, has_side_effects=True),
    )(start, soil, conductivity, storage, rain))


def solution(mesh):
    placed = (P("sec", "gx", None), P("sec", "gx", None), P(), P(), P(None, "gx", None))
    return jax.shard_map(
        functools.partial(body, mesh.shape["sec"], mesh.shape["gx"]),
        mesh=mesh,
        in_specs=placed,
        out_specs=(P("sec", "gx", None), P("sec", None, "gx", None)),
        check_vma=False,
    )
```

```python
import functools

import jax
import jax.numpy as jnp
from jax import lax
from jax.experimental import pallas as pl
from jax.experimental.pallas import tpu as pltpu
from jax.sharding import PartitionSpec as P


MESH = pl.DeviceIdType.MESH
RIM = 8
LANES = 128
ITERS = 4


def place_of(s):
    return s + s // 2 - 2 * (s // 3)


def coefficients(g, h):
    nu = [g[0], h[0]]
    for k in range(1, ITERS):
        nu.append(2.0 * g[k] - nu[0])
        nu.append(4.0 * h[k] - 2.0 * nu[1] - nu[2 * k - 1])

    def gram(i, j):
        return 0.5 * (nu[i + j] + nu[abs(i - j)])

    def gram_a(i, j):
        shifted = gram(i, 1) if j == 0 else 0.5 * (gram(i, j + 1) + gram(i, j - 1))
        return gram(i, j) - shifted

    G = [[gram(i, j) for j in range(ITERS)] for i in range(ITERS)]
    H = [[gram_a(max(i, j), min(i, j)) for j in range(ITERS)] for i in range(ITERS)]
    zero = jnp.zeros_like(g[0])

    def form(matrix, v, top):
        total = zero
        for i in range(top + 1):
            row = matrix[i][i] * v[i]
            for j in range(i):
                row = row + 2.0 * matrix[i][j] * v[j]
            total = total + row * v[i]
        return total

    z = [zero + 1.0] + [zero] * (ITERS - 1)
    p = list(z)
    x = [zero] * ITERS
    rz = nu[0]
    for k in range(ITERS):
        curve = form(H, p, k)
        alpha = jnp.where(curve > 0.0, rz / jnp.where(curve > 0.0, curve, 1.0), 0.0)
        x = [a + alpha * b for a, b in zip(x, p)]
        if k + 1 < ITERS:
            image = list(p)
            for i in range(k + 1):
                if i == 0:
                    image[1] = image[1] - p[0]
                else:
                    image[i + 1] = image[i + 1] - 0.5 * p[i]
                    image[i - 1] = image[i - 1] - 0.5 * p[i]
            z = [a - alpha * b for a, b in zip(z, image)]
            new = jnp.maximum(form(G, z, k + 1), 0.0)
            beta = jnp.where(rz > 0.0, new / jnp.where(rz > 0.0, rz, 1.0), 0.0)
            p = [a + beta * b for a, b in zip(z, p)]
            rz = new
    return x


def kernel(
    n_sec, n_gx, steps, kinds,
    start_ref, soil_ref, cond_ref, store_ref, rain_ref,
    out_ref, flow_ref,
    kind_mine, head, kind, store, cond, cap, face_l, face_r, face_c, diag, dinv, t0, t1, t2, t3,
    water, enter, leave, rainx, flows, pack_out, pack_in, landed, stats,
    own_sem, swap_send, swap_recv, col_send, col_recv, row_send, row_recv, land_send, land_recv,
    sum_send, sum_recv, flow_send, flow_recv, back_send, back_recv,
):
    f32 = jnp.float32
    layers, rows, wide = start_ref.shape
    cols = wide // n_sec
    total = layers * n_sec
    sec, gx = lax.axis_index("sec"), lax.axis_index("gx")
    here = place_of(sec)
    ext_r, ext_c = rows + 2 * RIM, cols + LANES
    own = (slice(0, rows), slice(0, cols))

    def at(place):
        return pl.ds(pl.multiple_of(place * cols, LANES), cols)

    def layers_of(s):
        return pl.ds(1 + s * layers, layers)

    plane = jnp.zeros((ext_r, ext_c), f32)
    for ref in (head, kind, cond, t0, t1, t2, t3, face_l):
        ref[0] = plane
        ref[total + 1] = plane

    def clear(l, carry):
        for ref in (head, kind):
            ref[l, rows:, :] = jnp.zeros((2 * RIM, ext_c), f32)
        return carry

    lax.fori_loop(1, total + 1, clear, 0)
    for c in range(steps):
        rainx[c] = plane
    pack_in[...] = jnp.zeros_like(pack_in)
    kind_mine[...] = soil_ref[...].astype(f32) + 1.0

    @pl.when(jnp.logical_or(gx == 0, gx == n_gx - 1))
    def _():
        def wipe(l, carry):
            for c in range(steps - 1):
                for k in range(ITERS):
                    for d in (0, 1):
                        landed[c, k, d, l] = jnp.zeros((RIM, cols), f32)
            return carry

        lax.fori_loop(0, total, wipe, 0)

    sec_peers = [lax.rem(sec + k, n_sec) for k in range(1, n_sec)]
    everyone = [
        {"sec": lax.rem(sec + i, n_sec), "gx": lax.rem(gx + j, n_gx)}
        for j in range(n_gx) for i in range(n_sec) if i + j
    ]
    barrier = pltpu.get_barrier_semaphore()
    for peer in everyone:
        pl.semaphore_signal(barrier, inc=1, device_id=peer, device_id_type=MESH)

    lane = lax.broadcasted_iota(jnp.int32, (ext_r, LANES), 1)
    after = pl.multiple_of(lax.rem(here + 1, n_sec) * cols, LANES)
    before = pl.multiple_of(lax.rem(here + n_sec - 1, n_sec) * cols + cols - LANES, LANES)
    for c in range(steps):
        rainx[c, 0:rows, 0:cols] = rain_ref[c, :, at(here)]
        rainx[c, 0:rows, cols:] = jnp.where(
            lane[0:rows] < LANES // 2, rain_ref[c, :, pl.ds(after, LANES)], rain_ref[c, :, pl.ds(before, LANES)]
        )
    pl.semaphore_wait(barrier, n_sec * n_gx - 1)

    swaps = []
    for f, (src, dst) in enumerate(((start_ref, head), (kind_mine, kind))):
        moves = []
        swaps.append(moves)
        copy = pltpu.make_async_copy(
            src.at[:, :, at(here)], dst.at[layers_of(sec), 0:rows, 0:cols], own_sem.at[f]
        )
        copy.start()
        moves.append(copy)
        for k, peer in enumerate(sec_peers):
            copy = pltpu.make_async_remote_copy(
                src_ref=src.at[:, :, at(place_of(peer))],
                dst_ref=dst.at[layers_of(sec), 0:rows, 0:cols],
                send_sem=swap_send.at[f, k],
                recv_sem=swap_recv.at[f, k],
                device_id={"sec": peer},
                device_id_type=MESH,
            )
            copy.start()
            moves.append(copy)

    def packed(field, low):
        outs = jnp.zeros((ext_r, LANES), f32)
        for l in range(total):
            if low:
                tile = field[1 + l, :, 0:LANES]
                shift = RIM * l
            else:
                tile = field[1 + l, :, cols - LANES:cols]
                shift = (RIM * l + RIM) % LANES
            moved = pltpu.roll(tile, shift, 1) if shift else tile
            outs = jnp.where(lane // RIM == l, moved, outs)
        return outs

    def send_cols(slot, field):
        pack_out[slot, 0] = packed(field, True)
        pack_out[slot, 1] = packed(field, False)
        for d in (0, 1):
            @pl.when(here > 0 if d == 0 else here < n_sec - 1)
            def _(d=d):
                col_copy(slot, d).start()

    def col_copy(slot, d):
        return pltpu.make_async_remote_copy(
            src_ref=pack_out.at[slot, d],
            dst_ref=pack_in.at[slot, d],
            send_sem=col_send.at[slot, d],
            recv_sem=col_recv.at[slot, d],
            device_id={"sec": place_of(lax.rem(here + n_sec - 1, n_sec) if d == 0 else lax.rem(here + 1, n_sec))},
            device_id_type=MESH,
        )

    def take_cols(slot, field):
        @pl.when(here > 0)
        def _():
            col_copy(slot, 0).wait_send()
            col_copy(slot, 1).wait_recv()

        @pl.when(here < n_sec - 1)
        def _():
            col_copy(slot, 1).wait_send()
            col_copy(slot, 0).wait_recv()

        right, left = pack_in[slot, 0], pack_in[slot, 1]
        for l in range(total):
            a, b = (-RIM * l) % LANES, (LANES - RIM - RIM * l) % LANES
            ra = pltpu.roll(right, a, 1) if a else right
            rb = pltpu.roll(left, b, 1) if b else left
            field[1 + l, :, cols:] = jnp.where(lane < RIM, ra, jnp.where(lane >= LANES - RIM, rb, 0.0))

    def row_copy(slot, field, first, count, width, d):
        src = pl.ds(0, RIM) if d == 0 else pl.ds(rows - RIM, RIM)
        dst = pl.ds(rows, RIM) if d == 0 else pl.ds(rows + RIM, RIM)
        return pltpu.make_async_remote_copy(
            src_ref=field.at[pl.ds(first, count), src, 0:width],
            dst_ref=field.at[pl.ds(first, count), dst, 0:width],
            send_sem=row_send.at[slot, d],
            recv_sem=row_recv.at[slot, d],
            device_id={"gx": lax.rem(gx + n_gx - 1, n_gx) if d == 0 else lax.rem(gx + 1, n_gx)},
            device_id_type=MESH,
        )

    def send_rows(*what):
        for d in (0, 1):
            @pl.when(gx > 0 if d == 0 else gx < n_gx - 1)
            def _(d=d):
                row_copy(*what, d).start()

    def take_rows(*what):
        @pl.when(gx > 0)
        def _():
            row_copy(*what, 0).wait_send()
            row_copy(*what, 1).wait_recv()

        @pl.when(gx < n_gx - 1)
        def _():
            row_copy(*what, 1).wait_send()
            row_copy(*what, 0).wait_recv()

    def shift(v, by, axis):
        return pltpu.roll(v, by % v.shape[axis], axis)

    def harmonic(a, b):
        return 2.0 * a * b / jnp.maximum(a + b, 1e-30)

    def folded(v):
        out = None
        for i in range(0, rows, RIM):
            for j in range(0, cols, LANES):
                part = v[i:i + RIM, j:j + LANES]
                out = part if out is None else out + part
        return out

    none = jnp.zeros((RIM, LANES), f32)
    basis = (t0, t1, t2, t3)

    outgoing = []
    for c in range(steps):
        if c == 0:
            fields = ((0, head, 1, total, cols), (1, kind, 1, total, cols), (2, rainx, 0, steps, ext_c))
            for f in range(2):
                for copy in swaps[f]:
                    copy.wait()
                send_rows(*fields[f])
            send_rows(*fields[2])
            take_rows(*fields[0])
            send_cols(c, head)
            take_rows(*fields[1])
            send_cols(steps, kind)
            take_rows(*fields[2])
            take_cols(steps, kind)

            def look(l, carry):
                here_kind = kind[l]
                a = jnp.zeros((ext_r, ext_c), f32)
                b = jnp.zeros((ext_r, ext_c), f32)
                for k in range(kinds):
                    same = here_kind == jnp.float32(k + 1)
                    a = jnp.where(same, cond_ref[k], a)
                    b = jnp.where(same, store_ref[k], b)
                kind[l] = a
                store[l] = b
                return carry

            lax.fori_loop(1, total + 1, look, 0)
        else:
            send_cols(c, head)
        take_cols(c, head)

        def soil(s, carry):
            amount = jnp.zeros((ext_r, ext_c), f32)
            for j in range(layers):
                l = 1 + s * layers + j
                sat = jax.nn.sigmoid(head[l])
                cond[l] = kind[l] * (0.05 + sat * sat)
                cap[l] = store[l] * (0.1 + sat * (1.0 - sat))
                amount = amount + sat
            water[s] = amount
            return carry

        lax.fori_loop(0, n_sec, soil, 0)

        depth = jnp.float32(layers)
        below = jnp.zeros((ext_r, ext_c), f32)
        for s in reversed(range(n_sec)):
            amount = water[s]
            water[s] = amount / depth * (0.5 + 0.5 * below / (below + depth))
            below = below + amount
        entering = rainx[c]
        for s in range(n_sec):
            enter[s] = entering
            flows[s, c] = entering[own]
            entering = water[s] * entering + 0.5 * cond[(s + 1) * layers]
            leave[s] = entering
        own_flow = pltpu.make_async_copy(flows.at[sec, c], flow_ref.at[0, c, :, at(here)], own_sem.at[3 + c])
        own_flow.start()
        late = [own_flow]
        for k, peer in enumerate(sec_peers):
            copy = pltpu.make_async_remote_copy(
                src_ref=flows.at[peer, c],
                dst_ref=flow_ref.at[0, c, :, at(here)],
                send_sem=flow_send.at[c, k],
                recv_sem=flow_recv.at[c, k],
                device_id={"sec": peer},
                device_id_type=MESH,
            )
            copy.start()
            late.append(copy)
        outgoing += late

        def faces(l, carry):
            k = cond[l]
            face_l[l] = harmonic(k, cond[l + 1])
            face_r[l] = harmonic(k, shift(k, -1, 0))
            face_c[l] = harmonic(k, shift(k, -1, 1))
            return carry

        lax.fori_loop(1, total + 1, faces, 0)

        def first(s, acc):
            for j in range(layers):
                l = 1 + s * layers + j
                up, down = face_l[l - 1], face_l[l]
                fr, fc = face_r[l], face_c[l]
                v = head[l]
                whole = cap[l] + up + down + fr + shift(fr, 1, 0) + fc + shift(fc, 1, 1)
                flux_r = fr * (shift(v, -1, 0) - v)
                flux_c = fc * (shift(v, -1, 1) - v)
                res = up - down + up * (head[l - 1] - v) + down * (head[l + 1] - v)
                res = res + flux_r - shift(flux_r, 1, 0) + flux_c - shift(flux_c, 1, 1)
                if j == 0:
                    res = res + enter[s]
                if j == layers - 1:
                    res = res - leave[s]
                inverse = jnp.where(whole > 0.0, 1.0 / jnp.maximum(whole, 1e-30), 0.0)
                z = res * inverse
                diag[l] = whole
                dinv[l] = inverse
                t0[l] = z
                acc = acc + folded(res * z)
            return acc

        def land_copy(k, d, c=c):
            src = pl.ds(0, RIM) if d == 0 else pl.ds(rows - RIM, RIM)
            return pltpu.make_async_remote_copy(
                src_ref=basis[k].at[pl.ds(1, total), src, 0:cols],
                dst_ref=landed.at[c, k, d],
                send_sem=land_send.at[c, k, d],
                recv_sem=land_recv.at[c, k, d],
                device_id={"gx": lax.rem(gx + n_gx - 1, n_gx) if d == 0 else lax.rem(gx + 1, n_gx)},
                device_id_type=MESH,
            )

        def send_land(k):
            if c + 1 < steps:
                for d in (0, 1):
                    @pl.when(gx > 0 if d == 0 else gx < n_gx - 1)
                    def _(d=d):
                        land_copy(k, d).start()

        g = [lax.fori_loop(0, n_sec, first, none)]
        send_land(0)
        h = []
        for k in range(ITERS):
            def apply(l, acc, k=k):
                t = basis[k]
                fr, fc = face_r[l], face_c[l]
                v = t[l]
                near = face_l[l - 1] * t[l - 1] + face_l[l] * t[l + 1]
                near = near + fr * shift(v, -1, 0) + shift(fr * v, 1, 0)
                near = near + fc * shift(v, -1, 1) + shift(fc * v, 1, 1)
                ah = acc[0] + folded(v * near)
                ag = acc[1]
                if k + 1 < ITERS:
                    new = dinv[l] * near
                    if k > 0:
                        new = 2.0 * new - basis[k - 1][l]
                    basis[k + 1][l] = new
                    ag = ag + folded(diag[l] * new * new)
                return (ah, ag)

            ah, ag = lax.fori_loop(1, total + 1, apply, (none, none))
            h.append(ah)
            if k + 1 < ITERS:
                g.append(ag)
                send_land(k + 1)

        flat = jnp.concatenate([jnp.sum(v, axis=0, keepdims=True) for v in g + h], axis=0)
        part = LANES // (2 * ITERS)
        by = LANES // 2
        while by >= part:
            flat = flat + pltpu.roll(flat, by, 1)
            by //= 2
        which = lax.broadcasted_iota(jnp.int32, flat.shape, 0)
        group = lax.broadcasted_iota(jnp.int32, flat.shape, 1) // part
        mine = sec * n_gx + gx
        stats[c, mine] = jnp.sum(jnp.where(which == group, flat, 0.0), axis=0, keepdims=True)
        sends = []
        for k, peer in enumerate(everyone):
            copy = pltpu.make_async_remote_copy(
                src_ref=stats.at[c, mine],
                dst_ref=stats.at[c, mine],
                send_sem=sum_send.at[c, k],
                recv_sem=sum_recv.at[c, k],
                device_id=peer,
                device_id_type=MESH,
            )
            copy.start()
            sends.append(copy)
        for copy in sends:
            copy.wait()
        summed = stats[c, 0]
        for k in range(1, n_sec * n_gx):
            summed = summed + stats[c, k]
        parts = [
            jnp.sum(jnp.where(group[0:1] == k, summed, 0.0), axis=1, keepdims=True)
            for k in range(2 * ITERS)
        ]
        x = coefficients(parts[:ITERS], parts[ITERS:])
        x = [jnp.broadcast_to(v, (rows, cols)) for v in x]

        def update(l, carry):
            v = head[l, 0:rows, 0:cols]
            for k in range(ITERS):
                v = v + x[k] * basis[k][l, 0:rows, 0:cols]
            head[l, 0:rows, 0:cols] = v
            return carry

        lax.fori_loop(1, total + 1, update, 0)
        if c + 1 < steps:
            for d in (0, 1):
                @pl.when(gx > 0 if d == 0 else gx < n_gx - 1)
                def _(d=d):
                    for k in range(ITERS):
                        land_copy(k, d).wait_send()

                @pl.when(gx < n_gx - 1 if d == 0 else gx > 0)
                def _(d=d):
                    for k in range(ITERS):
                        land_copy(k, d).wait_recv()

            def update_rim(l, carry):
                for d in (0, 1):
                    at_rows = slice(rows + d * RIM, rows + d * RIM + RIM)
                    v = head[l, at_rows, 0:cols]
                    for k in range(ITERS):
                        v = v + x[k][0:RIM] * landed[c, k, d, l - 1]
                    head[l, at_rows, 0:cols] = v
                return carry

            lax.fori_loop(1, total + 1, update_rim, 0)

    copy = pltpu.make_async_copy(head.at[layers_of(sec), 0:rows, 0:cols], out_ref.at[:, :, at(here)], own_sem.at[2])
    copy.start()
    outgoing.append(copy)
    for k, peer in enumerate(sec_peers):
        copy = pltpu.make_async_remote_copy(
            src_ref=head.at[layers_of(peer), 0:rows, 0:cols],
            dst_ref=out_ref.at[:, :, at(here)],
            send_sem=back_send.at[k],
            recv_sem=back_recv.at[k],
            device_id={"sec": peer},
            device_id_type=MESH,
        )
        copy.start()
        outgoing.append(copy)
    for copy in outgoing:
        copy.wait()


def body(n_sec, n_gx, start, soil, conductivity, storage, rain):
    layers, rows, wide = start.shape
    steps = rain.shape[0]
    cols = wide // n_sec
    total = layers * n_sec
    assert total * RIM <= LANES and cols % LANES == 0 and rows % RIM == 0 and n_sec == 4
    ext = (rows + 2 * RIM, cols + LANES)
    f32 = jnp.float32
    field = pltpu.VMEM((total + 2,) + ext, f32)
    per_sec = pltpu.VMEM((n_sec,) + ext, f32)
    dma = pltpu.SemaphoreType.DMA
    vmem = pl.BlockSpec(memory_space=pltpu.VMEM)
    smem = pl.BlockSpec(memory_space=pltpu.SMEM)
    return tuple(pl.pallas_call(
        functools.partial(kernel, n_sec, n_gx, steps, conductivity.shape[0]),
        out_shape=(
            jax.ShapeDtypeStruct(start.shape, f32),
            jax.ShapeDtypeStruct((1, steps, rows, wide), f32),
        ),
        in_specs=[vmem, vmem, smem, smem, vmem],
        out_specs=(vmem, vmem),
        scratch_shapes=[pltpu.VMEM(start.shape, f32)]
        + [field] * 14
        + [per_sec] * 3
        + [
            pltpu.VMEM((steps,) + ext, f32),
            pltpu.VMEM((n_sec, steps, rows, cols), f32),
            pltpu.VMEM((steps + 1, 2, ext[0], LANES), f32),
            pltpu.VMEM((steps + 1, 2, ext[0], LANES), f32),
            pltpu.VMEM((steps, ITERS, 2, total, RIM, cols), f32),
            pltpu.VMEM((steps, n_sec * n_gx, 1, LANES), f32),
            dma((3 + steps,)),
            dma((2, n_sec - 1)),
            dma((2, n_sec - 1)),
            dma((steps + 1, 2)),
            dma((steps + 1, 2)),
            dma((3, 2)),
            dma((3, 2)),
            dma((steps, ITERS, 2)),
            dma((steps, ITERS, 2)),
            dma((steps, n_sec * n_gx)),
            dma((steps, n_sec * n_gx)),
            dma((steps, n_sec - 1)),
            dma((steps, n_sec - 1)),
            dma((n_sec - 1,)),
            dma((n_sec - 1,)),
        ],
        compiler_params=pltpu.CompilerParams(collective_id=0, has_side_effects=True),
    )(start, soil, conductivity, storage, rain))


def solution(mesh):
    placed = (P("sec", "gx", None), P("sec", "gx", None), P(), P(), P(None, "gx", None))
    return jax.shard_map(
        functools.partial(body, mesh.shape["sec"], mesh.shape["gx"]),
        mesh=mesh,
        in_specs=placed,
        out_specs=(P("sec", "gx", None), P("sec", None, "gx", None)),
        check_vma=False,
    )
```

```python
import functools

import jax
import jax.numpy as jnp
from jax import lax
from jax.experimental import pallas as pl
from jax.experimental.pallas import tpu as pltpu
from jax.sharding import PartitionSpec as P


MESH = pl.DeviceIdType.MESH
RIM = 8
LANES = 128
ITERS = 4


def place_of(s):
    return s + s // 2 - 2 * (s // 3)


def coefficients(g, h):
    nu = [g[0], h[0]]
    for k in range(1, ITERS):
        nu.append(2.0 * g[k] - nu[0])
        nu.append(4.0 * h[k] - 2.0 * nu[1] - nu[2 * k - 1])

    def gram(i, j):
        return 0.5 * (nu[i + j] + nu[abs(i - j)])

    def gram_a(i, j):
        shifted = gram(i, 1) if j == 0 else 0.5 * (gram(i, j + 1) + gram(i, j - 1))
        return gram(i, j) - shifted

    G = [[gram(i, j) for j in range(ITERS)] for i in range(ITERS)]
    H = [[gram_a(max(i, j), min(i, j)) for j in range(ITERS)] for i in range(ITERS)]
    zero = jnp.zeros_like(g[0])

    def form(matrix, v, top):
        total = zero
        for i in range(top + 1):
            row = matrix[i][i] * v[i]
            for j in range(i):
                row = row + 2.0 * matrix[i][j] * v[j]
            total = total + row * v[i]
        return total

    z = [zero + 1.0] + [zero] * (ITERS - 1)
    p = list(z)
    x = [zero] * ITERS
    rz = nu[0]
    for k in range(ITERS):
        curve = form(H, p, k)
        alpha = jnp.where(curve > 0.0, rz / jnp.where(curve > 0.0, curve, 1.0), 0.0)
        x = [a + alpha * b for a, b in zip(x, p)]
        if k + 1 < ITERS:
            image = list(p)
            for i in range(k + 1):
                if i == 0:
                    image[1] = image[1] - p[0]
                else:
                    image[i + 1] = image[i + 1] - 0.5 * p[i]
                    image[i - 1] = image[i - 1] - 0.5 * p[i]
            z = [a - alpha * b for a, b in zip(z, image)]
            new = jnp.maximum(form(G, z, k + 1), 0.0)
            beta = jnp.where(rz > 0.0, new / jnp.where(rz > 0.0, rz, 1.0), 0.0)
            p = [a + beta * b for a, b in zip(z, p)]
            rz = new
    return x


def kernel(
    n_sec, n_gx, steps, kinds,
    start_ref, soil_ref, cond_ref, store_ref, rain_ref,
    out_ref, flow_ref,
    head, soils, kind, store, cond, cap, face_l, face_r, face_c, diag, dinv, t0, t1, t2, t3,
    water, enter, leave, rainx, flows, pack_out, pack_in, soil_out, soil_in, landed, stats,
    met_sem, own_sem, swap_send, swap_recv, col_send, col_recv, row_send, row_recv, land_send, land_recv,
    sum_send, sum_recv, flow_send, flow_recv, back_send, back_recv,
):
    f32 = jnp.float32
    layers, rows, wide = start_ref.shape
    cols = wide // n_sec
    total = layers * n_sec
    sec, gx = lax.axis_index("sec"), lax.axis_index("gx")
    here = place_of(sec)
    ext_r, ext_c = rows + 2 * RIM, cols + LANES
    own = (slice(0, rows), slice(0, cols))

    def at(place):
        return pl.ds(pl.multiple_of(place * cols, LANES), cols)

    def layers_of(s):
        return pl.ds(1 + s * layers, layers)

    sec_peers = [lax.rem(sec + k, n_sec) for k in range(1, n_sec)]
    gx_peers = [lax.rem(gx + k, n_gx) for k in range(1, n_gx)]
    everyone = [
        {"sec": lax.rem(sec + i, n_sec), "gx": lax.rem(gx + j, n_gx)}
        for j in range(n_gx) for i in range(n_sec) if i + j
    ]
    barrier = pltpu.get_barrier_semaphore()
    for peer in sec_peers:
        pl.semaphore_signal(barrier, inc=1, device_id={"sec": peer}, device_id_type=MESH)
    for peer in gx_peers:
        pl.semaphore_signal(barrier, inc=1, device_id={"gx": peer}, device_id_type=MESH)

    plane = jnp.zeros((ext_r, ext_c), f32)
    for ref in (head, cond, t0, t1, t2, t3, face_l):
        ref[0] = plane
        ref[total + 1] = plane
    for d in (0, 1):
        rim = slice(rows + d * RIM, rows + d * RIM + RIM)

        @pl.when(gx == n_gx - 1 if d == 0 else gx == 0)
        def _(d=d, rim=rim):
            def wipe(l, carry):
                head[l + 1, rim, :] = jnp.zeros((RIM, ext_c), f32)
                soils[l + 1, rim, :] = jnp.zeros((RIM, ext_c), jnp.int32)
                for c in range(steps - 1):
                    for k in range(ITERS):
                        landed[c, k, d, l] = jnp.zeros((RIM, cols), f32)
                return carry

            lax.fori_loop(0, total, wipe, 0)
            for c in range(steps):
                rainx[c, rim, :] = jnp.zeros((RIM, ext_c), f32)

        @pl.when(here == n_sec - 1 if d == 0 else here == 0)
        def _(d=d):
            for c in range(steps):
                pack_in[c, d] = jnp.zeros((ext_r, LANES), f32)
            soil_in[d] = jnp.zeros((ext_r, LANES), jnp.int32)

    at_row = lax.broadcasted_iota(jnp.int32, (ext_r, ext_c), 0)
    at_col = lax.broadcasted_iota(jnp.int32, (ext_r, ext_c), 1)
    outside = (at_col >= cols + RIM) & (at_col < ext_c - RIM)
    outside = outside | ((at_row >= rows) & (at_row < rows + RIM) & (gx == n_gx - 1))
    outside = outside | ((at_row >= rows + RIM) & (gx == 0))
    outside = outside | ((at_col >= cols) & (at_col < cols + RIM) & (here == n_sec - 1))
    outside = outside | ((at_col >= ext_c - RIM) & (here == 0))

    lane = lax.broadcasted_iota(jnp.int32, (ext_r, LANES), 1)
    after = pl.multiple_of(lax.rem(here + 1, n_sec) * cols, LANES)
    before = pl.multiple_of(lax.rem(here + n_sec - 1, n_sec) * cols + cols - LANES, LANES)
    for c in range(steps):
        rainx[c, 0:rows, 0:cols] = rain_ref[c, :, at(here)]
        rainx[c, 0:rows, cols:] = jnp.where(
            lane[0:rows] < LANES // 2, rain_ref[c, :, pl.ds(after, LANES)], rain_ref[c, :, pl.ds(before, LANES)]
        )
    pl.semaphore_wait(barrier, n_sec + n_gx - 2)
    for peer in sec_peers:
        pl.semaphore_signal(met_sem, inc=1, device_id={"sec": peer}, device_id_type=MESH)

    swaps = []
    for f, (src, dst) in enumerate(((start_ref, head), (soil_ref, soils))):
        moves = []
        swaps.append(moves)
        copy = pltpu.make_async_copy(
            src.at[:, :, at(here)], dst.at[layers_of(sec), 0:rows, 0:cols], own_sem.at[f]
        )
        copy.start()
        moves.append(copy)
        for k, peer in enumerate(sec_peers):
            copy = pltpu.make_async_remote_copy(
                src_ref=src.at[:, :, at(place_of(peer))],
                dst_ref=dst.at[layers_of(sec), 0:rows, 0:cols],
                send_sem=swap_send.at[f, k],
                recv_sem=swap_recv.at[f, k],
                device_id={"sec": peer},
                device_id_type=MESH,
            )
            copy.start()
            moves.append(copy)

    def packed(field, low):
        outs = jnp.zeros((ext_r, LANES), field.dtype)
        for l in range(total):
            if low:
                tile = field[1 + l, :, 0:LANES]
                shift = RIM * l
            else:
                tile = field[1 + l, :, cols - LANES:cols]
                shift = (RIM * l + RIM) % LANES
            moved = pltpu.roll(tile, shift, 1) if shift else tile
            outs = jnp.where(lane // RIM == l, moved, outs)
        return outs

    def send_cols(slot, field):
        out, _ = packs(slot)
        out[0] = packed(field, True)
        out[1] = packed(field, False)
        for d in (0, 1):
            @pl.when(here > 0 if d == 0 else here < n_sec - 1)
            def _(d=d):
                col_copy(slot, d).start()

    def packs(slot):
        return (pack_out.at[slot], pack_in.at[slot]) if slot < steps else (soil_out, soil_in)

    def col_copy(slot, d):
        return pltpu.make_async_remote_copy(
            src_ref=packs(slot)[0].at[d],
            dst_ref=packs(slot)[1].at[d],
            send_sem=col_send.at[slot, d],
            recv_sem=col_recv.at[slot, d],
            device_id={"sec": place_of(lax.rem(here + n_sec - 1, n_sec) if d == 0 else lax.rem(here + 1, n_sec))},
            device_id_type=MESH,
        )

    def take_cols(slot, field):
        @pl.when(here > 0)
        def _():
            col_copy(slot, 0).wait_send()
            col_copy(slot, 1).wait_recv()

        @pl.when(here < n_sec - 1)
        def _():
            col_copy(slot, 1).wait_send()
            col_copy(slot, 0).wait_recv()

        taken = packs(slot)[1]
        right, left, nil = taken[0], taken[1], jnp.zeros((ext_r, LANES), field.dtype)
        for l in range(total):
            a, b = (-RIM * l) % LANES, (LANES - RIM - RIM * l) % LANES
            ra = pltpu.roll(right, a, 1) if a else right
            rb = pltpu.roll(left, b, 1) if b else left
            field[1 + l, :, cols:] = jnp.where(lane < RIM, ra, jnp.where(lane >= LANES - RIM, rb, nil))

    def row_copy(slot, field, first, count, width, d):
        src = pl.ds(0, RIM) if d == 0 else pl.ds(rows - RIM, RIM)
        dst = pl.ds(rows, RIM) if d == 0 else pl.ds(rows + RIM, RIM)
        return pltpu.make_async_remote_copy(
            src_ref=field.at[pl.ds(first, count), src, 0:width],
            dst_ref=field.at[pl.ds(first, count), dst, 0:width],
            send_sem=row_send.at[slot, d],
            recv_sem=row_recv.at[slot, d],
            device_id={"gx": lax.rem(gx + n_gx - 1, n_gx) if d == 0 else lax.rem(gx + 1, n_gx)},
            device_id_type=MESH,
        )

    def send_rows(*what):
        for d in (0, 1):
            @pl.when(gx > 0 if d == 0 else gx < n_gx - 1)
            def _(d=d):
                row_copy(*what, d).start()

    def take_rows(*what):
        @pl.when(gx > 0)
        def _():
            row_copy(*what, 0).wait_send()
            row_copy(*what, 1).wait_recv()

        @pl.when(gx < n_gx - 1)
        def _():
            row_copy(*what, 1).wait_send()
            row_copy(*what, 0).wait_recv()

    def shift(v, by, axis):
        return pltpu.roll(v, by % v.shape[axis], axis)

    def harmonic(a, b):
        return 2.0 * a * b / jnp.maximum(a + b, 1e-30)

    def folded(v):
        out = None
        for i in range(0, rows, RIM):
            for j in range(0, cols, LANES):
                part = v[i:i + RIM, j:j + LANES]
                out = part if out is None else out + part
        return out

    none = jnp.zeros((RIM, LANES), f32)
    basis = (t0, t1, t2, t3)

    outgoing = []
    for c in range(steps):
        if c == 0:
            fields = ((0, head, 1, total, cols), (1, soils, 1, total, cols), (2, rainx, 0, steps, ext_c))
            for f in range(2):
                for copy in swaps[f]:
                    copy.wait()
                send_rows(*fields[f])
            send_rows(*fields[2])
            take_rows(*fields[0])
            send_cols(c, head)
            take_rows(*fields[1])
            send_cols(steps, soils)
            take_rows(*fields[2])
            take_cols(steps, soils)

            spot = lax.broadcasted_iota(jnp.int32, (ext_r, LANES), 1)
            of_cond = jnp.zeros((ext_r, LANES), f32)
            of_store = jnp.zeros((ext_r, LANES), f32)
            for k in range(kinds):
                of_cond = jnp.where(spot == k, cond_ref[k], of_cond)
                of_store = jnp.where(spot == k, store_ref[k], of_store)

            def look(l, carry):
                for j in range(0, ext_c, LANES):
                    which = soils[l, :, j:j + LANES]
                    hide = outside[:, j:j + LANES]
                    a = jnp.take_along_axis(of_cond, which, axis=1, mode="promise_in_bounds")
                    b = jnp.take_along_axis(of_store, which, axis=1, mode="promise_in_bounds")
                    kind[l, :, j:j + LANES] = jnp.where(hide, 0.0, a)
                    store[l, :, j:j + LANES] = jnp.where(hide, 0.0, b)
                return carry

            lax.fori_loop(1, total + 1, look, 0)
        else:
            send_cols(c, head)
        take_cols(c, head)

        def soil(s, carry):
            amount = jnp.zeros((ext_r, ext_c), f32)
            for j in range(layers):
                l = 1 + s * layers + j
                sat = jax.nn.sigmoid(head[l])
                cond[l] = kind[l] * (0.05 + sat * sat)
                cap[l] = store[l] * (0.1 + sat * (1.0 - sat))
                amount = amount + sat
            water[s] = amount
            return carry

        lax.fori_loop(0, n_sec, soil, 0)

        depth = jnp.float32(layers)
        below = jnp.zeros((ext_r, ext_c), f32)
        for s in reversed(range(n_sec)):
            amount = water[s]
            water[s] = amount / depth * (0.5 + 0.5 * below / (below + depth))
            below = below + amount
        entering = rainx[c]
        for s in range(n_sec):
            enter[s] = entering
            flows[s, c] = entering[own]
            entering = water[s] * entering + 0.5 * cond[(s + 1) * layers]
            leave[s] = entering
        own_flow = pltpu.make_async_copy(flows.at[sec, c], flow_ref.at[0, c, :, at(here)], own_sem.at[3 + c])
        own_flow.start()
        late = [own_flow]
        for k, peer in enumerate(sec_peers):
            copy = pltpu.make_async_remote_copy(
                src_ref=flows.at[peer, c],
                dst_ref=flow_ref.at[0, c, :, at(here)],
                send_sem=flow_send.at[c, k],
                recv_sem=flow_recv.at[c, k],
                device_id={"sec": peer},
                device_id_type=MESH,
            )
            copy.start()
            late.append(copy)
        outgoing += late

        def faces(l, carry):
            k = cond[l]
            face_l[l] = harmonic(k, cond[l + 1])
            face_r[l] = harmonic(k, shift(k, -1, 0))
            face_c[l] = harmonic(k, shift(k, -1, 1))
            return carry

        lax.fori_loop(1, total + 1, faces, 0)

        def first(s, acc):
            for j in range(layers):
                l = 1 + s * layers + j
                up, down = face_l[l - 1], face_l[l]
                fr, fc = face_r[l], face_c[l]
                v = head[l]
                whole = cap[l] + up + down + fr + shift(fr, 1, 0) + fc + shift(fc, 1, 1)
                flux_r = fr * (shift(v, -1, 0) - v)
                flux_c = fc * (shift(v, -1, 1) - v)
                res = up - down + up * (head[l - 1] - v) + down * (head[l + 1] - v)
                res = res + flux_r - shift(flux_r, 1, 0) + flux_c - shift(flux_c, 1, 1)
                if j == 0:
                    res = res + enter[s]
                if j == layers - 1:
                    res = res - leave[s]
                inverse = jnp.where(whole > 0.0, 1.0 / jnp.maximum(whole, 1e-30), 0.0)
                z = res * inverse
                diag[l] = whole
                dinv[l] = inverse
                t0[l] = z
                acc = acc + folded(res * z)
            return acc

        def land_copy(k, d, c=c):
            src = pl.ds(0, RIM) if d == 0 else pl.ds(rows - RIM, RIM)
            return pltpu.make_async_remote_copy(
                src_ref=basis[k].at[pl.ds(1, total), src, 0:cols],
                dst_ref=landed.at[c, k, d],
                send_sem=land_send.at[c, k, d],
                recv_sem=land_recv.at[c, k, d],
                device_id={"gx": lax.rem(gx + n_gx - 1, n_gx) if d == 0 else lax.rem(gx + 1, n_gx)},
                device_id_type=MESH,
            )

        def send_land(k):
            if c + 1 < steps:
                for d in (0, 1):
                    @pl.when(gx > 0 if d == 0 else gx < n_gx - 1)
                    def _(d=d):
                        land_copy(k, d).start()

        g = [lax.fori_loop(0, n_sec, first, none)]
        send_land(0)
        h = []
        for k in range(ITERS):
            def apply(l, acc, k=k):
                t = basis[k]
                fr, fc = face_r[l], face_c[l]
                v = t[l]
                near = face_l[l - 1] * t[l - 1] + face_l[l] * t[l + 1]
                near = near + fr * shift(v, -1, 0) + shift(fr * v, 1, 0)
                near = near + fc * shift(v, -1, 1) + shift(fc * v, 1, 1)
                ah = acc[0] + folded(v * near)
                ag = acc[1]
                if k + 1 < ITERS:
                    new = dinv[l] * near
                    if k > 0:
                        new = 2.0 * new - basis[k - 1][l]
                    basis[k + 1][l] = new
                    ag = ag + folded(diag[l] * new * new)
                return (ah, ag)

            ah, ag = lax.fori_loop(1, total + 1, apply, (none, none))
            h.append(ah)
            if k + 1 < ITERS:
                g.append(ag)
                send_land(k + 1)

        flat = jnp.concatenate([jnp.sum(v, axis=0, keepdims=True) for v in g + h], axis=0)
        part = LANES // (2 * ITERS)
        by = LANES // 2
        while by >= part:
            flat = flat + pltpu.roll(flat, by, 1)
            by //= 2
        which = lax.broadcasted_iota(jnp.int32, flat.shape, 0)
        group = lax.broadcasted_iota(jnp.int32, flat.shape, 1) // part
        mine = sec * n_gx + gx
        stats[c, mine] = jnp.sum(jnp.where(which == group, flat, 0.0), axis=0, keepdims=True)
        if c == 0:
            pl.semaphore_wait(met_sem, n_sec - 1)
        sends = []
        for k, peer in enumerate(everyone):
            copy = pltpu.make_async_remote_copy(
                src_ref=stats.at[c, mine],
                dst_ref=stats.at[c, mine],
                send_sem=sum_send.at[c, k],
                recv_sem=sum_recv.at[c, k],
                device_id=peer,
                device_id_type=MESH,
            )
            copy.start()
            sends.append(copy)
        for copy in sends:
            copy.wait()
        summed = stats[c, 0]
        for k in range(1, n_sec * n_gx):
            summed = summed + stats[c, k]
        parts = [
            jnp.sum(jnp.where(group[0:1] == k, summed, 0.0), axis=1, keepdims=True)
            for k in range(2 * ITERS)
        ]
        x = coefficients(parts[:ITERS], parts[ITERS:])
        x = [jnp.broadcast_to(v, (rows, cols)) for v in x]

        def update(l, carry):
            v = head[l, 0:rows, 0:cols]
            for k in range(ITERS):
                v = v + x[k] * basis[k][l, 0:rows, 0:cols]
            head[l, 0:rows, 0:cols] = v
            return carry

        lax.fori_loop(1, total + 1, update, 0)
        if c + 1 < steps:
            for d in (0, 1):
                @pl.when(gx > 0 if d == 0 else gx < n_gx - 1)
                def _(d=d):
                    for k in range(ITERS):
                        land_copy(k, d).wait_send()

                @pl.when(gx < n_gx - 1 if d == 0 else gx > 0)
                def _(d=d):
                    for k in range(ITERS):
                        land_copy(k, d).wait_recv()

            def update_rim(l, carry):
                for d in (0, 1):
                    at_rows = slice(rows + d * RIM, rows + d * RIM + RIM)
                    v = head[l, at_rows, 0:cols]
                    for k in range(ITERS):
                        v = v + x[k][0:RIM] * landed[c, k, d, l - 1]
                    head[l, at_rows, 0:cols] = v
                return carry

            lax.fori_loop(1, total + 1, update_rim, 0)

    copy = pltpu.make_async_copy(head.at[layers_of(sec), 0:rows, 0:cols], out_ref.at[:, :, at(here)], own_sem.at[2])
    copy.start()
    outgoing.append(copy)
    for k, peer in enumerate(sec_peers):
        copy = pltpu.make_async_remote_copy(
            src_ref=head.at[layers_of(peer), 0:rows, 0:cols],
            dst_ref=out_ref.at[:, :, at(here)],
            send_sem=back_send.at[k],
            recv_sem=back_recv.at[k],
            device_id={"sec": peer},
            device_id_type=MESH,
        )
        copy.start()
        outgoing.append(copy)
    for copy in outgoing:
        copy.wait()


def body(n_sec, n_gx, start, soil, conductivity, storage, rain):
    layers, rows, wide = start.shape
    steps = rain.shape[0]
    cols = wide // n_sec
    total = layers * n_sec
    assert total * RIM <= LANES and cols % LANES == 0 and rows % RIM == 0 and n_sec == 4
    ext = (rows + 2 * RIM, cols + LANES)
    f32 = jnp.float32
    field = pltpu.VMEM((total + 2,) + ext, f32)
    per_sec = pltpu.VMEM((n_sec,) + ext, f32)
    dma = pltpu.SemaphoreType.DMA
    vmem = pl.BlockSpec(memory_space=pltpu.VMEM)
    hbm = pl.BlockSpec(memory_space=pl.ANY)
    smem = pl.BlockSpec(memory_space=pltpu.SMEM)
    return tuple(pl.pallas_call(
        functools.partial(kernel, n_sec, n_gx, steps, conductivity.shape[0]),
        out_shape=(
            jax.ShapeDtypeStruct(start.shape, f32),
            jax.ShapeDtypeStruct((1, steps, rows, wide), f32),
        ),
        in_specs=[hbm, hbm, smem, smem, vmem],
        out_specs=(hbm, hbm),
        scratch_shapes=[field, pltpu.VMEM((total + 2,) + ext, jnp.int32)]
        + [field] * 13
        + [per_sec] * 3
        + [
            pltpu.VMEM((steps,) + ext, f32),
            pltpu.VMEM((n_sec, steps, rows, cols), f32),
            pltpu.VMEM((steps, 2, ext[0], LANES), f32),
            pltpu.VMEM((steps, 2, ext[0], LANES), f32),
            pltpu.VMEM((2, ext[0], LANES), jnp.int32),
            pltpu.VMEM((2, ext[0], LANES), jnp.int32),
            pltpu.VMEM((steps, ITERS, 2, total, RIM, cols), f32),
            pltpu.VMEM((steps, n_sec * n_gx, 1, LANES), f32),
            pltpu.SemaphoreType.REGULAR,
            dma((3 + steps,)),
            dma((2, n_sec - 1)),
            dma((2, n_sec - 1)),
            dma((steps + 1, 2)),
            dma((steps + 1, 2)),
            dma((3, 2)),
            dma((3, 2)),
            dma((steps, ITERS, 2)),
            dma((steps, ITERS, 2)),
            dma((steps, n_sec * n_gx)),
            dma((steps, n_sec * n_gx)),
            dma((steps, n_sec - 1)),
            dma((steps, n_sec - 1)),
            dma((n_sec - 1,)),
            dma((n_sec - 1,)),
        ],
        compiler_params=pltpu.CompilerParams(collective_id=0, has_side_effects=True),
    )(start, soil, conductivity, storage, rain))


def solution(mesh):
    placed = (P("sec", "gx", None), P("sec", "gx", None), P(), P(), P(None, "gx", None))
    return jax.shard_map(
        functools.partial(body, mesh.shape["sec"], mesh.shape["gx"]),
        mesh=mesh,
        in_specs=placed,
        out_specs=(P("sec", "gx", None), P("sec", None, "gx", None)),
        check_vma=False,
    )
```

```python
import functools

import jax
import jax.numpy as jnp
from jax import lax
from jax.experimental import pallas as pl
from jax.experimental.pallas import tpu as pltpu
from jax.sharding import PartitionSpec as P


MESH = pl.DeviceIdType.MESH
RIM = 8
LANES = 128
ITERS = 4


def place_of(s):
    return s + s // 2 - 2 * (s // 3)


def coefficients(g, h):
    nu = [g[0], h[0]]
    for k in range(1, ITERS):
        nu.append(2.0 * g[k] - nu[0])
        nu.append(4.0 * h[k] - 2.0 * nu[1] - nu[2 * k - 1])

    def gram(i, j):
        return 0.5 * (nu[i + j] + nu[abs(i - j)])

    def gram_a(i, j):
        shifted = gram(i, 1) if j == 0 else 0.5 * (gram(i, j + 1) + gram(i, j - 1))
        return gram(i, j) - shifted

    G = [[gram(i, j) for j in range(ITERS)] for i in range(ITERS)]
    H = [[gram_a(max(i, j), min(i, j)) for j in range(ITERS)] for i in range(ITERS)]
    zero = jnp.zeros_like(g[0])

    def form(matrix, v, top):
        total = zero
        for i in range(top + 1):
            row = matrix[i][i] * v[i]
            for j in range(i):
                row = row + 2.0 * matrix[i][j] * v[j]
            total = total + row * v[i]
        return total

    z = [zero + 1.0] + [zero] * (ITERS - 1)
    p = list(z)
    x = [zero] * ITERS
    rz = nu[0]
    for k in range(ITERS):
        curve = form(H, p, k)
        alpha = jnp.where(curve > 0.0, rz / jnp.where(curve > 0.0, curve, 1.0), 0.0)
        x = [a + alpha * b for a, b in zip(x, p)]
        if k + 1 < ITERS:
            image = list(p)
            for i in range(k + 1):
                if i == 0:
                    image[1] = image[1] - p[0]
                else:
                    image[i + 1] = image[i + 1] - 0.5 * p[i]
                    image[i - 1] = image[i - 1] - 0.5 * p[i]
            z = [a - alpha * b for a, b in zip(z, image)]
            new = jnp.maximum(form(G, z, k + 1), 0.0)
            beta = jnp.where(rz > 0.0, new / jnp.where(rz > 0.0, rz, 1.0), 0.0)
            p = [a + beta * b for a, b in zip(z, p)]
            rz = new
    return x


def kernel(
    n_sec, n_gx, steps, kinds,
    start_ref, soil_ref, cond_ref, store_ref, rain_ref,
    out_ref, flow_ref,
    head, soils, kind, store, cond, cap, face_l, face_r, face_c, diag, dinv, t0, t1, t2, t3,
    water, enter, leave, rainx, flows, pack_out, pack_in, soil_out, soil_in, landed, stats,
    met_sem, own_sem, swap_send, swap_recv, col_send, col_recv, row_send, row_recv, land_send, land_recv,
    sum_send, sum_recv, flow_send, flow_recv, back_send, back_recv,
):
    f32 = jnp.float32
    layers, rows, wide = start_ref.shape
    cols = wide // n_sec
    total = layers * n_sec
    sec, gx = lax.axis_index("sec"), lax.axis_index("gx")
    here = place_of(sec)
    ext_r, ext_c = rows + 2 * RIM, cols + LANES
    own = (slice(0, rows), slice(0, cols))

    def at(place):
        return pl.ds(pl.multiple_of(place * cols, LANES), cols)

    def layers_of(s):
        return pl.ds(1 + s * layers, layers)

    sec_peers = [lax.rem(sec + k, n_sec) for k in range(1, n_sec)]
    gx_peers = [lax.rem(gx + k, n_gx) for k in range(1, n_gx)]
    everyone = [
        {"sec": lax.rem(sec + i, n_sec), "gx": lax.rem(gx + j, n_gx)}
        for j in range(n_gx) for i in range(n_sec) if i + j
    ]
    barrier = pltpu.get_barrier_semaphore()
    for peer in sec_peers:
        pl.semaphore_signal(barrier, inc=1, device_id={"sec": peer}, device_id_type=MESH)
    for peer in gx_peers:
        pl.semaphore_signal(barrier, inc=1, device_id={"gx": peer}, device_id_type=MESH)

    plane = jnp.zeros((ext_r, ext_c), f32)
    for ref in (head, cond, t0, t1, t2, t3, face_l):
        ref[0] = plane
        ref[total + 1] = plane
    for d in (0, 1):
        rim = slice(rows + d * RIM, rows + d * RIM + RIM)

        @pl.when(gx == n_gx - 1 if d == 0 else gx == 0)
        def _(d=d, rim=rim):
            def wipe(l, carry):
                head[l + 1, rim, :] = jnp.zeros((RIM, ext_c), f32)
                soils[l + 1, rim, :] = jnp.zeros((RIM, ext_c), jnp.int32)
                for c in range(steps - 1):
                    for k in range(ITERS):
                        landed[c, k, d, l] = jnp.zeros((RIM, cols), f32)
                return carry

            lax.fori_loop(0, total, wipe, 0)
            for c in range(steps):
                rainx[c, rim, :] = jnp.zeros((RIM, ext_c), f32)

        @pl.when(here == n_sec - 1 if d == 0 else here == 0)
        def _(d=d):
            for c in range(steps):
                pack_in[c, d] = jnp.zeros((ext_r, LANES), f32)
            soil_in[d] = jnp.zeros((ext_r, LANES), jnp.int32)

    at_row = lax.broadcasted_iota(jnp.int32, (ext_r, ext_c), 0)
    at_col = lax.broadcasted_iota(jnp.int32, (ext_r, ext_c), 1)
    outside = (at_col >= cols + RIM) & (at_col < ext_c - RIM)
    outside = outside | ((at_row >= rows) & (at_row < rows + RIM) & (gx == n_gx - 1))
    outside = outside | ((at_row >= rows + RIM) & (gx == 0))
    outside = outside | ((at_col >= cols) & (at_col < cols + RIM) & (here == n_sec - 1))
    outside = outside | ((at_col >= ext_c - RIM) & (here == 0))

    lane = lax.broadcasted_iota(jnp.int32, (ext_r, LANES), 1)
    after = pl.multiple_of(lax.rem(here + 1, n_sec) * cols, LANES)
    before = pl.multiple_of(lax.rem(here + n_sec - 1, n_sec) * cols + cols - LANES, LANES)
    for c in range(steps):
        rainx[c, 0:rows, 0:cols] = rain_ref[c, :, at(here)]
        rainx[c, 0:rows, cols:] = jnp.where(
            lane[0:rows] < LANES // 2, rain_ref[c, :, pl.ds(after, LANES)], rain_ref[c, :, pl.ds(before, LANES)]
        )
    pl.semaphore_wait(barrier, n_sec + n_gx - 2)
    for peer in sec_peers:
        pl.semaphore_signal(met_sem, inc=1, device_id={"sec": peer}, device_id_type=MESH)

    swaps = []
    for f, (src, dst) in enumerate(((start_ref, head), (soil_ref, soils))):
        moves = []
        swaps.append(moves)
        copy = pltpu.make_async_copy(
            src.at[:, :, at(here)], dst.at[layers_of(sec), 0:rows, 0:cols], own_sem.at[f]
        )
        copy.start()
        moves.append(copy)
        for k, peer in enumerate(sec_peers):
            copy = pltpu.make_async_remote_copy(
                src_ref=src.at[:, :, at(place_of(peer))],
                dst_ref=dst.at[layers_of(sec), 0:rows, 0:cols],
                send_sem=swap_send.at[f, k],
                recv_sem=swap_recv.at[f, k],
                device_id={"sec": peer},
                device_id_type=MESH,
            )
            copy.start()
            moves.append(copy)

    def packed(field, low):
        outs = jnp.zeros((ext_r, LANES), field.dtype)
        for l in range(total):
            if low:
                tile = field[1 + l, :, 0:LANES]
                shift = RIM * l
            else:
                tile = field[1 + l, :, cols - LANES:cols]
                shift = (RIM * l + RIM) % LANES
            moved = pltpu.roll(tile, shift, 1) if shift else tile
            outs = jnp.where(lane // RIM == l, moved, outs)
        return outs

    def send_cols(slot, field):
        out, _ = packs(slot)
        out[0] = packed(field, True)
        out[1] = packed(field, False)
        for d in (0, 1):
            @pl.when(here > 0 if d == 0 else here < n_sec - 1)
            def _(d=d):
                col_copy(slot, d).start()

    def packs(slot):
        return (pack_out.at[slot], pack_in.at[slot]) if slot < steps else (soil_out, soil_in)

    def col_copy(slot, d):
        return pltpu.make_async_remote_copy(
            src_ref=packs(slot)[0].at[d],
            dst_ref=packs(slot)[1].at[d],
            send_sem=col_send.at[slot, d],
            recv_sem=col_recv.at[slot, d],
            device_id={"sec": place_of(lax.rem(here + n_sec - 1, n_sec) if d == 0 else lax.rem(here + 1, n_sec))},
            device_id_type=MESH,
        )

    def take_cols(slot, field):
        @pl.when(here > 0)
        def _():
            col_copy(slot, 0).wait_send()
            col_copy(slot, 1).wait_recv()

        @pl.when(here < n_sec - 1)
        def _():
            col_copy(slot, 1).wait_send()
            col_copy(slot, 0).wait_recv()

        taken = packs(slot)[1]
        right, left, nil = taken[0], taken[1], jnp.zeros((ext_r, LANES), field.dtype)
        for l in range(total):
            a, b = (-RIM * l) % LANES, (LANES - RIM - RIM * l) % LANES
            ra = pltpu.roll(right, a, 1) if a else right
            rb = pltpu.roll(left, b, 1) if b else left
            field[1 + l, :, cols:] = jnp.where(lane < RIM, ra, jnp.where(lane >= LANES - RIM, rb, nil))

    def row_copy(slot, field, first, count, width, d):
        src = pl.ds(0, RIM) if d == 0 else pl.ds(rows - RIM, RIM)
        dst = pl.ds(rows, RIM) if d == 0 else pl.ds(rows + RIM, RIM)
        return pltpu.make_async_remote_copy(
            src_ref=field.at[pl.ds(first, count), src, 0:width],
            dst_ref=field.at[pl.ds(first, count), dst, 0:width],
            send_sem=row_send.at[slot, d],
            recv_sem=row_recv.at[slot, d],
            device_id={"gx": lax.rem(gx + n_gx - 1, n_gx) if d == 0 else lax.rem(gx + 1, n_gx)},
            device_id_type=MESH,
        )

    def send_rows(*what):
        for d in (0, 1):
            @pl.when(gx > 0 if d == 0 else gx < n_gx - 1)
            def _(d=d):
                row_copy(*what, d).start()

    def take_rows(*what):
        @pl.when(gx > 0)
        def _():
            row_copy(*what, 0).wait_send()
            row_copy(*what, 1).wait_recv()

        @pl.when(gx < n_gx - 1)
        def _():
            row_copy(*what, 1).wait_send()
            row_copy(*what, 0).wait_recv()

    def shift(v, by, axis):
        return pltpu.roll(v, by % v.shape[axis], axis)

    def harmonic(a, b):
        return 2.0 * a * b / jnp.maximum(a + b, 1e-30)

    def folded(v):
        out = None
        for i in range(0, rows, RIM):
            for j in range(0, cols, LANES):
                part = v[i:i + RIM, j:j + LANES]
                out = part if out is None else out + part
        return out

    none = jnp.zeros((RIM, LANES), f32)
    basis = (t0, t1, t2, t3)

    def back_copy(k, peer):
        return pltpu.make_async_remote_copy(
            src_ref=head.at[layers_of(peer), 0:rows, 0:cols],
            dst_ref=out_ref.at[:, :, at(here)],
            send_sem=back_send.at[k],
            recv_sem=back_recv.at[k],
            device_id={"sec": peer},
            device_id_type=MESH,
        )

    outgoing = []
    for c in range(steps):
        if c == 0:
            fields = ((0, head, 1, total, cols), (1, soils, 1, total, cols), (2, rainx, 0, steps, ext_c))
            for f in range(2):
                for copy in swaps[f]:
                    copy.wait()
                send_rows(*fields[f])
            send_rows(*fields[2])
            take_rows(*fields[0])
            send_cols(c, head)
            take_rows(*fields[1])
            send_cols(steps, soils)
            take_rows(*fields[2])

            spot = lax.broadcasted_iota(jnp.int32, (ext_r, LANES), 1)
            of_cond = jnp.zeros((ext_r, LANES), f32)
            of_store = jnp.zeros((ext_r, LANES), f32)
            for k in range(kinds):
                of_cond = jnp.where(spot == k, cond_ref[k], of_cond)
                of_store = jnp.where(spot == k, store_ref[k], of_store)

            def look(lanes, l, carry):
                for j in range(lanes.start, lanes.stop, LANES):
                    which = soils[l, :, j:j + LANES]
                    hide = outside[:, j:j + LANES]
                    a = jnp.take_along_axis(of_cond, which, axis=1, mode="promise_in_bounds")
                    b = jnp.take_along_axis(of_store, which, axis=1, mode="promise_in_bounds")
                    kind[l, :, j:j + LANES] = jnp.where(hide, 0.0, a)
                    store[l, :, j:j + LANES] = jnp.where(hide, 0.0, b)
                return carry

        else:
            send_cols(c, head)

        def soil(lanes, s, carry):
            amount = jnp.zeros((ext_r, lanes.stop - lanes.start), f32)
            for j in range(layers):
                l = 1 + s * layers + j
                sat = jax.nn.sigmoid(head[l, :, lanes])
                cond[l, :, lanes] = kind[l, :, lanes] * (0.05 + sat * sat)
                cap[l, :, lanes] = store[l, :, lanes] * (0.1 + sat * (1.0 - sat))
                amount = amount + sat
            water[s, :, lanes] = amount
            return carry

        def couple(lanes):
            depth = jnp.float32(layers)
            below = jnp.zeros((ext_r, lanes.stop - lanes.start), f32)
            slopes = [None] * n_sec
            for s in reversed(range(n_sec)):
                amount = water[s, :, lanes]
                slopes[s] = amount / depth * (0.5 + 0.5 * below / (below + depth))
                below = below + amount
            entering = rainx[c, :, lanes]
            for s in range(n_sec):
                enter[s, :, lanes] = entering
                if lanes.start == 0:
                    flows[s, c] = entering[own]
                entering = slopes[s] * entering + 0.5 * cond[(s + 1) * layers, :, lanes]
                leave[s, :, lanes] = entering

        def faces(lanes, l, carry):
            k = cond[l, :, lanes]
            face_l[l, :, lanes] = harmonic(k, cond[l + 1, :, lanes])
            face_r[l, :, lanes] = harmonic(k, shift(k, -1, 0))
            return carry

        def faces_across(l, carry):
            k = cond[l]
            face_c[l] = harmonic(k, shift(k, -1, 1))
            return carry

        def prepare(lanes):
            if c == 0:
                lax.fori_loop(1, total + 1, functools.partial(look, lanes), 0)
            lax.fori_loop(0, n_sec, functools.partial(soil, lanes), 0)
            couple(lanes)
            lax.fori_loop(1, total + 1, functools.partial(faces, lanes), 0)

        prepare(slice(0, cols))
        own_flow = pltpu.make_async_copy(flows.at[sec, c], flow_ref.at[0, c, :, at(here)], own_sem.at[3 + c])
        own_flow.start()
        late = [own_flow]
        for k, peer in enumerate(sec_peers):
            copy = pltpu.make_async_remote_copy(
                src_ref=flows.at[peer, c],
                dst_ref=flow_ref.at[0, c, :, at(here)],
                send_sem=flow_send.at[c, k],
                recv_sem=flow_recv.at[c, k],
                device_id={"sec": peer},
                device_id_type=MESH,
            )
            copy.start()
            late.append(copy)
        outgoing += late

        if c == 0:
            take_cols(steps, soils)
        take_cols(c, head)
        prepare(slice(cols, ext_c))
        lax.fori_loop(1, total + 1, faces_across, 0)

        def first(s, acc):
            for j in range(layers):
                l = 1 + s * layers + j
                up, down = face_l[l - 1], face_l[l]
                fr, fc = face_r[l], face_c[l]
                v = head[l]
                whole = cap[l] + up + down + fr + shift(fr, 1, 0) + fc + shift(fc, 1, 1)
                flux_r = fr * (shift(v, -1, 0) - v)
                flux_c = fc * (shift(v, -1, 1) - v)
                res = up - down + up * (head[l - 1] - v) + down * (head[l + 1] - v)
                res = res + flux_r - shift(flux_r, 1, 0) + flux_c - shift(flux_c, 1, 1)
                if j == 0:
                    res = res + enter[s]
                if j == layers - 1:
                    res = res - leave[s]
                inverse = jnp.where(whole > 0.0, 1.0 / jnp.maximum(whole, 1e-30), 0.0)
                z = res * inverse
                diag[l] = whole
                dinv[l] = inverse
                t0[l] = z
                acc = acc + folded(res * z)
            return acc

        def land_copy(k, d, c=c):
            src = pl.ds(0, RIM) if d == 0 else pl.ds(rows - RIM, RIM)
            return pltpu.make_async_remote_copy(
                src_ref=basis[k].at[pl.ds(1, total), src, 0:cols],
                dst_ref=landed.at[c, k, d],
                send_sem=land_send.at[c, k, d],
                recv_sem=land_recv.at[c, k, d],
                device_id={"gx": lax.rem(gx + n_gx - 1, n_gx) if d == 0 else lax.rem(gx + 1, n_gx)},
                device_id_type=MESH,
            )

        def send_land(k):
            if c + 1 < steps:
                for d in (0, 1):
                    @pl.when(gx > 0 if d == 0 else gx < n_gx - 1)
                    def _(d=d):
                        land_copy(k, d).start()

        g = [lax.fori_loop(0, n_sec, first, none)]
        send_land(0)
        h = []
        for k in range(ITERS):
            def apply(l, acc, k=k):
                t = basis[k]
                fr, fc = face_r[l], face_c[l]
                v = t[l]
                near = face_l[l - 1] * t[l - 1] + face_l[l] * t[l + 1]
                near = near + fr * shift(v, -1, 0) + shift(fr * v, 1, 0)
                near = near + fc * shift(v, -1, 1) + shift(fc * v, 1, 1)
                ah = acc[0] + folded(v * near)
                ag = acc[1]
                if k + 1 < ITERS:
                    new = dinv[l] * near
                    if k > 0:
                        new = 2.0 * new - basis[k - 1][l]
                    basis[k + 1][l] = new
                    ag = ag + folded(diag[l] * new * new)
                return (ah, ag)

            ah, ag = lax.fori_loop(1, total + 1, apply, (none, none))
            h.append(ah)
            if k + 1 < ITERS:
                g.append(ag)
                send_land(k + 1)

        flat = jnp.concatenate([jnp.sum(v, axis=0, keepdims=True) for v in g + h], axis=0)
        part = LANES // (2 * ITERS)
        by = LANES // 2
        while by >= part:
            flat = flat + pltpu.roll(flat, by, 1)
            by //= 2
        which = lax.broadcasted_iota(jnp.int32, flat.shape, 0)
        group = lax.broadcasted_iota(jnp.int32, flat.shape, 1) // part
        mine = sec * n_gx + gx
        stats[c, mine] = jnp.sum(jnp.where(which == group, flat, 0.0), axis=0, keepdims=True)
        if c == 0:
            pl.semaphore_wait(met_sem, n_sec - 1)
        sends = []
        for k, peer in enumerate(everyone):
            copy = pltpu.make_async_remote_copy(
                src_ref=stats.at[c, mine],
                dst_ref=stats.at[c, mine],
                send_sem=sum_send.at[c, k],
                recv_sem=sum_recv.at[c, k],
                device_id=peer,
                device_id_type=MESH,
            )
            copy.start()
            sends.append(copy)
        for copy in sends:
            copy.wait()
        summed = stats[c, 0]
        for k in range(1, n_sec * n_gx):
            summed = summed + stats[c, k]
        parts = [
            jnp.sum(jnp.where(group[0:1] == k, summed, 0.0), axis=1, keepdims=True)
            for k in range(2 * ITERS)
        ]
        x = coefficients(parts[:ITERS], parts[ITERS:])
        x = [jnp.broadcast_to(v, (rows, cols)) for v in x]

        def update(l, carry):
            v = head[l, 0:rows, 0:cols]
            for k in range(ITERS):
                v = v + x[k] * basis[k][l, 0:rows, 0:cols]
            head[l, 0:rows, 0:cols] = v
            return carry

        if c + 1 == steps:
            for i in range(1, n_sec):
                peer = sec_peers[i - 1]
                lax.fori_loop(1 + peer * layers, 1 + (peer + 1) * layers, update, 0)
                back_copy(i - 1, peer).start()
                outgoing.append(back_copy(i - 1, peer))
            lax.fori_loop(1 + sec * layers, 1 + (sec + 1) * layers, update, 0)
        else:
            lax.fori_loop(1, total + 1, update, 0)
        if c + 1 < steps:
            for d in (0, 1):
                @pl.when(gx > 0 if d == 0 else gx < n_gx - 1)
                def _(d=d):
                    for k in range(ITERS):
                        land_copy(k, d).wait_send()

                @pl.when(gx < n_gx - 1 if d == 0 else gx > 0)
                def _(d=d):
                    for k in range(ITERS):
                        land_copy(k, d).wait_recv()

            def update_rim(l, carry):
                for d in (0, 1):
                    at_rows = slice(rows + d * RIM, rows + d * RIM + RIM)
                    v = head[l, at_rows, 0:cols]
                    for k in range(ITERS):
                        v = v + x[k][0:RIM] * landed[c, k, d, l - 1]
                    head[l, at_rows, 0:cols] = v
                return carry

            lax.fori_loop(1, total + 1, update_rim, 0)

    copy = pltpu.make_async_copy(head.at[layers_of(sec), 0:rows, 0:cols], out_ref.at[:, :, at(here)], own_sem.at[2])
    copy.start()
    outgoing.append(copy)
    for copy in outgoing:
        copy.wait()


def body(n_sec, n_gx, start, soil, conductivity, storage, rain):
    layers, rows, wide = start.shape
    steps = rain.shape[0]
    cols = wide // n_sec
    total = layers * n_sec
    assert total * RIM <= LANES and cols % LANES == 0 and rows % RIM == 0 and n_sec == 4
    ext = (rows + 2 * RIM, cols + LANES)
    f32 = jnp.float32
    field = pltpu.VMEM((total + 2,) + ext, f32)
    per_sec = pltpu.VMEM((n_sec,) + ext, f32)
    dma = pltpu.SemaphoreType.DMA
    vmem = pl.BlockSpec(memory_space=pltpu.VMEM)
    hbm = pl.BlockSpec(memory_space=pl.ANY)
    smem = pl.BlockSpec(memory_space=pltpu.SMEM)
    return tuple(pl.pallas_call(
        functools.partial(kernel, n_sec, n_gx, steps, conductivity.shape[0]),
        out_shape=(
            jax.ShapeDtypeStruct(start.shape, f32),
            jax.ShapeDtypeStruct((1, steps, rows, wide), f32),
        ),
        in_specs=[hbm, hbm, smem, smem, vmem],
        out_specs=(hbm, hbm),
        scratch_shapes=[field, pltpu.VMEM((total + 2,) + ext, jnp.int32)]
        + [field] * 13
        + [per_sec] * 3
        + [
            pltpu.VMEM((steps,) + ext, f32),
            pltpu.VMEM((n_sec, steps, rows, cols), f32),
            pltpu.VMEM((steps, 2, ext[0], LANES), f32),
            pltpu.VMEM((steps, 2, ext[0], LANES), f32),
            pltpu.VMEM((2, ext[0], LANES), jnp.int32),
            pltpu.VMEM((2, ext[0], LANES), jnp.int32),
            pltpu.VMEM((steps, ITERS, 2, total, RIM, cols), f32),
            pltpu.VMEM((steps, n_sec * n_gx, 1, LANES), f32),
            pltpu.SemaphoreType.REGULAR,
            dma((3 + steps,)),
            dma((2, n_sec - 1)),
            dma((2, n_sec - 1)),
            dma((steps + 1, 2)),
            dma((steps + 1, 2)),
            dma((3, 2)),
            dma((3, 2)),
            dma((steps, ITERS, 2)),
            dma((steps, ITERS, 2)),
            dma((steps, n_sec * n_gx)),
            dma((steps, n_sec * n_gx)),
            dma((steps, n_sec - 1)),
            dma((steps, n_sec - 1)),
            dma((n_sec - 1,)),
            dma((n_sec - 1,)),
        ],
        compiler_params=pltpu.CompilerParams(collective_id=0, has_side_effects=True),
    )(start, soil, conductivity, storage, rain))


def solution(mesh):
    placed = (P("sec", "gx", None), P("sec", "gx", None), P(), P(), P(None, "gx", None))
    return jax.shard_map(
        functools.partial(body, mesh.shape["sec"], mesh.shape["gx"]),
        mesh=mesh,
        in_specs=placed,
        out_specs=(P("sec", "gx", None), P("sec", None, "gx", None)),
        check_vma=False,
    )
```

```python
import functools

import jax
import jax.numpy as jnp
from jax import lax
from jax.experimental import pallas as pl
from jax.experimental.pallas import tpu as pltpu
from jax.sharding import PartitionSpec as P


MESH = pl.DeviceIdType.MESH
RIM = 8
LANES = 128
ITERS = 4


def place_of(s):
    return s + s // 2 - 2 * (s // 3)


def coefficients(g, h):
    nu = [g[0], h[0]]
    for k in range(1, ITERS):
        nu.append(2.0 * g[k] - nu[0])
        nu.append(4.0 * h[k] - 2.0 * nu[1] - nu[2 * k - 1])

    def gram(i, j):
        return 0.5 * (nu[i + j] + nu[abs(i - j)])

    def gram_a(i, j):
        shifted = gram(i, 1) if j == 0 else 0.5 * (gram(i, j + 1) + gram(i, j - 1))
        return gram(i, j) - shifted

    G = [[gram(i, j) for j in range(ITERS)] for i in range(ITERS)]
    H = [[gram_a(max(i, j), min(i, j)) for j in range(ITERS)] for i in range(ITERS)]
    zero = jnp.zeros_like(g[0])

    def form(matrix, v, top):
        total = zero
        for i in range(top + 1):
            row = matrix[i][i] * v[i]
            for j in range(i):
                row = row + 2.0 * matrix[i][j] * v[j]
            total = total + row * v[i]
        return total

    z = [zero + 1.0] + [zero] * (ITERS - 1)
    p = list(z)
    x = [zero] * ITERS
    rz = nu[0]
    for k in range(ITERS):
        curve = form(H, p, k)
        alpha = jnp.where(curve > 0.0, rz / jnp.where(curve > 0.0, curve, 1.0), 0.0)
        x = [a + alpha * b for a, b in zip(x, p)]
        if k + 1 < ITERS:
            image = list(p)
            for i in range(k + 1):
                if i == 0:
                    image[1] = image[1] - p[0]
                else:
                    image[i + 1] = image[i + 1] - 0.5 * p[i]
                    image[i - 1] = image[i - 1] - 0.5 * p[i]
            z = [a - alpha * b for a, b in zip(z, image)]
            new = jnp.maximum(form(G, z, k + 1), 0.0)
            beta = jnp.where(rz > 0.0, new / jnp.where(rz > 0.0, rz, 1.0), 0.0)
            p = [a + beta * b for a, b in zip(z, p)]
            rz = new
    return x


def kernel(
    n_sec, n_gx, steps, kinds,
    start_ref, soil_ref, cond_ref, store_ref, rain_ref,
    out_ref, flow_ref,
    head, soils, kind, store, cond, cap, face_l, face_r, face_c, diag, dinv, t0, t1, t2, t3,
    water, enter, leave, rainx, flows, pack_out, pack_in, soil_out, soil_in, landed, stats,
    met_sem, own_sem, swap_send, swap_recv, col_send, col_recv, row_send, row_recv, land_send, land_recv,
    sum_send, sum_recv, flow_send, flow_recv, back_send, back_recv,
):
    f32 = jnp.float32
    layers, rows, wide = start_ref.shape
    cols = wide // n_sec
    total = layers * n_sec
    sec, gx = lax.axis_index("sec"), lax.axis_index("gx")
    here = place_of(sec)
    ext_r, ext_c = rows + 2 * RIM, cols + LANES
    own = (slice(0, rows), slice(0, cols))

    def at(place):
        return pl.ds(pl.multiple_of(place * cols, LANES), cols)

    def layers_of(s):
        return pl.ds(1 + s * layers, layers)

    sec_peers = [lax.rem(sec + k, n_sec) for k in range(1, n_sec)]
    gx_peers = [lax.rem(gx + k, n_gx) for k in range(1, n_gx)]
    everyone = [
        {"sec": lax.rem(sec + i, n_sec), "gx": lax.rem(gx + j, n_gx)}
        for j in range(n_gx) for i in range(n_sec) if i + j
    ]
    barrier = pltpu.get_barrier_semaphore()
    for peer in sec_peers:
        pl.semaphore_signal(barrier, inc=1, device_id={"sec": peer}, device_id_type=MESH)
    for peer in gx_peers:
        pl.semaphore_signal(barrier, inc=1, device_id={"gx": peer}, device_id_type=MESH)

    plane = jnp.zeros((ext_r, ext_c), f32)
    for ref in (head, cond, t0, t1, t2, t3, face_l):
        ref[0] = plane
        ref[total + 1] = plane
    for d in (0, 1):
        rim = slice(rows + d * RIM, rows + d * RIM + RIM)

        @pl.when(gx == n_gx - 1 if d == 0 else gx == 0)
        def _(d=d, rim=rim):
            def wipe(l, carry):
                head[l + 1, rim, :] = jnp.zeros((RIM, ext_c), f32)
                soils[l + 1, rim, :] = jnp.zeros((RIM, ext_c), jnp.int32)
                for c in range(steps - 1):
                    for k in range(ITERS):
                        landed[c, k, d, l] = jnp.zeros((RIM, cols), f32)
                return carry

            lax.fori_loop(0, total, wipe, 0)
            for c in range(steps):
                rainx[c, rim, :] = jnp.zeros((RIM, ext_c), f32)

        @pl.when(here == n_sec - 1 if d == 0 else here == 0)
        def _(d=d):
            for c in range(steps):
                pack_in[c, d] = jnp.zeros((ext_r, LANES), f32)
            soil_in[d] = jnp.zeros((ext_r, LANES), jnp.int32)

    at_row = lax.broadcasted_iota(jnp.int32, (ext_r, ext_c), 0)
    at_col = lax.broadcasted_iota(jnp.int32, (ext_r, ext_c), 1)
    outside = (at_col >= cols + RIM) & (at_col < ext_c - RIM)
    outside = outside | ((at_row >= rows) & (at_row < rows + RIM) & (gx == n_gx - 1))
    outside = outside | ((at_row >= rows + RIM) & (gx == 0))
    outside = outside | ((at_col >= cols) & (at_col < cols + RIM) & (here == n_sec - 1))
    outside = outside | ((at_col >= ext_c - RIM) & (here == 0))

    lane = lax.broadcasted_iota(jnp.int32, (ext_r, LANES), 1)
    after = pl.multiple_of(lax.rem(here + 1, n_sec) * cols, LANES)
    before = pl.multiple_of(lax.rem(here + n_sec - 1, n_sec) * cols + cols - LANES, LANES)
    for c in range(steps):
        rainx[c, 0:rows, 0:cols] = rain_ref[c, :, at(here)]
        rainx[c, 0:rows, cols:] = jnp.where(
            lane[0:rows] < LANES // 2, rain_ref[c, :, pl.ds(after, LANES)], rain_ref[c, :, pl.ds(before, LANES)]
        )
    pl.semaphore_wait(barrier, n_sec + n_gx - 2)
    for peer in sec_peers:
        pl.semaphore_signal(met_sem, inc=1, device_id={"sec": peer}, device_id_type=MESH)

    swaps = []
    for f, (src, dst) in enumerate(((start_ref, head), (soil_ref, soils))):
        moves = []
        swaps.append(moves)
        copy = pltpu.make_async_copy(
            src.at[:, :, at(here)], dst.at[layers_of(sec), 0:rows, 0:cols], own_sem.at[f]
        )
        copy.start()
        moves.append(copy)
        for k, peer in enumerate(sec_peers):
            copy = pltpu.make_async_remote_copy(
                src_ref=src.at[:, :, at(place_of(peer))],
                dst_ref=dst.at[layers_of(sec), 0:rows, 0:cols],
                send_sem=swap_send.at[f, k],
                recv_sem=swap_recv.at[f, k],
                device_id={"sec": peer},
                device_id_type=MESH,
            )
            copy.start()
            moves.append(copy)

    def packed(field, low):
        outs = jnp.zeros((ext_r, LANES), field.dtype)
        for l in range(total):
            if low:
                tile = field[1 + l, :, 0:LANES]
                shift = RIM * l
            else:
                tile = field[1 + l, :, cols - LANES:cols]
                shift = (RIM * l + RIM) % LANES
            moved = pltpu.roll(tile, shift, 1) if shift else tile
            outs = jnp.where(lane // RIM == l, moved, outs)
        return outs

    def send_cols(slot, field):
        out, _ = packs(slot)
        for d in (0, 1):
            out[d] = packed(field, d == 0)

            @pl.when(here > 0 if d == 0 else here < n_sec - 1)
            def _(d=d):
                col_copy(slot, d).start()

    def packs(slot):
        return (pack_out.at[slot], pack_in.at[slot]) if slot < steps else (soil_out, soil_in)

    def col_copy(slot, d):
        return pltpu.make_async_remote_copy(
            src_ref=packs(slot)[0].at[d],
            dst_ref=packs(slot)[1].at[d],
            send_sem=col_send.at[slot, d],
            recv_sem=col_recv.at[slot, d],
            device_id={"sec": place_of(lax.rem(here + n_sec - 1, n_sec) if d == 0 else lax.rem(here + 1, n_sec))},
            device_id_type=MESH,
        )

    def take_cols(slot, field):
        @pl.when(here > 0)
        def _():
            col_copy(slot, 0).wait_send()
            col_copy(slot, 1).wait_recv()

        @pl.when(here < n_sec - 1)
        def _():
            col_copy(slot, 1).wait_send()
            col_copy(slot, 0).wait_recv()

        taken = packs(slot)[1]
        right, left, nil = taken[0], taken[1], jnp.zeros((ext_r, LANES), field.dtype)
        for l in range(total):
            a, b = (-RIM * l) % LANES, (LANES - RIM - RIM * l) % LANES
            ra = pltpu.roll(right, a, 1) if a else right
            rb = pltpu.roll(left, b, 1) if b else left
            field[1 + l, :, cols:] = jnp.where(lane < RIM, ra, jnp.where(lane >= LANES - RIM, rb, nil))

    def row_copy(slot, field, first, count, width, d):
        src = pl.ds(0, RIM) if d == 0 else pl.ds(rows - RIM, RIM)
        dst = pl.ds(rows, RIM) if d == 0 else pl.ds(rows + RIM, RIM)
        return pltpu.make_async_remote_copy(
            src_ref=field.at[pl.ds(first, count), src, 0:width],
            dst_ref=field.at[pl.ds(first, count), dst, 0:width],
            send_sem=row_send.at[slot, d],
            recv_sem=row_recv.at[slot, d],
            device_id={"gx": lax.rem(gx + n_gx - 1, n_gx) if d == 0 else lax.rem(gx + 1, n_gx)},
            device_id_type=MESH,
        )

    def send_rows(*what):
        for d in (0, 1):
            @pl.when(gx > 0 if d == 0 else gx < n_gx - 1)
            def _(d=d):
                row_copy(*what, d).start()

    def take_rows(*what):
        @pl.when(gx > 0)
        def _():
            row_copy(*what, 0).wait_send()
            row_copy(*what, 1).wait_recv()

        @pl.when(gx < n_gx - 1)
        def _():
            row_copy(*what, 1).wait_send()
            row_copy(*what, 0).wait_recv()

    def shift(v, by, axis):
        return pltpu.roll(v, by % v.shape[axis], axis)

    def harmonic(a, b):
        return 2.0 * a * b / jnp.maximum(a + b, 1e-30)

    def folded(v):
        out = None
        for i in range(0, rows, RIM):
            for j in range(0, cols, LANES):
                part = v[i:i + RIM, j:j + LANES]
                out = part if out is None else out + part
        return out

    none = jnp.zeros((RIM, LANES), f32)
    basis = (t0, t1, t2, t3)

    def back_copy(k, peer):
        return pltpu.make_async_remote_copy(
            src_ref=head.at[layers_of(peer), 0:rows, 0:cols],
            dst_ref=out_ref.at[:, :, at(here)],
            send_sem=back_send.at[k],
            recv_sem=back_recv.at[k],
            device_id={"sec": peer},
            device_id_type=MESH,
        )

    outgoing = []
    for c in range(steps):
        if c == 0:
            fields = ((0, head, 1, total, cols), (1, soils, 1, total, cols), (2, rainx, 0, steps, ext_c))
            for f in range(2):
                for copy in swaps[f]:
                    copy.wait()
                send_rows(*fields[f])
            send_rows(*fields[2])
            take_rows(*fields[0])
            send_cols(c, head)
            take_rows(*fields[1])
            send_cols(steps, soils)
            take_rows(*fields[2])

            spot = lax.broadcasted_iota(jnp.int32, (ext_r, LANES), 1)
            of_cond = jnp.zeros((ext_r, LANES), f32)
            of_store = jnp.zeros((ext_r, LANES), f32)
            for k in range(kinds):
                of_cond = jnp.where(spot == k, cond_ref[k], of_cond)
                of_store = jnp.where(spot == k, store_ref[k], of_store)

            def look(lanes, l, carry):
                for j in range(lanes.start, lanes.stop, LANES):
                    which = soils[l, :, j:j + LANES]
                    hide = outside[:, j:j + LANES]
                    a = jnp.take_along_axis(of_cond, which, axis=1, mode="promise_in_bounds")
                    b = jnp.take_along_axis(of_store, which, axis=1, mode="promise_in_bounds")
                    kind[l, :, j:j + LANES] = jnp.where(hide, 0.0, a)
                    store[l, :, j:j + LANES] = jnp.where(hide, 0.0, b)
                return carry

        else:
            send_cols(c, head)

        def soil(lanes, s, carry):
            amount = jnp.zeros((ext_r, lanes.stop - lanes.start), f32)
            for j in range(layers):
                l = 1 + s * layers + j
                sat = jax.nn.sigmoid(head[l, :, lanes])
                cond[l, :, lanes] = kind[l, :, lanes] * (0.05 + sat * sat)
                cap[l, :, lanes] = store[l, :, lanes] * (0.1 + sat * (1.0 - sat))
                amount = amount + sat
            water[s, :, lanes] = amount
            return carry

        def couple(lanes):
            depth = jnp.float32(layers)
            below = jnp.zeros((ext_r, lanes.stop - lanes.start), f32)
            slopes = [None] * n_sec
            for s in reversed(range(n_sec)):
                amount = water[s, :, lanes]
                slopes[s] = amount / depth * (0.5 + 0.5 * below / (below + depth))
                below = below + amount
            entering = rainx[c, :, lanes]
            for s in range(n_sec):
                enter[s, :, lanes] = entering
                if lanes.start == 0:
                    flows[s, c] = entering[own]
                entering = slopes[s] * entering + 0.5 * cond[(s + 1) * layers, :, lanes]
                leave[s, :, lanes] = entering

        def faces(lanes, l, carry):
            k = cond[l, :, lanes]
            face_l[l, :, lanes] = harmonic(k, cond[l + 1, :, lanes])
            face_r[l, :, lanes] = harmonic(k, shift(k, -1, 0))
            return carry

        def faces_across(l, carry):
            k = cond[l]
            face_c[l] = harmonic(k, shift(k, -1, 1))
            return carry

        def prepare(lanes):
            if c == 0:
                lax.fori_loop(1, total + 1, functools.partial(look, lanes), 0)
            lax.fori_loop(0, n_sec, functools.partial(soil, lanes), 0)
            couple(lanes)
            lax.fori_loop(1, total + 1, functools.partial(faces, lanes), 0)

        prepare(slice(0, cols))
        own_flow = pltpu.make_async_copy(flows.at[sec, c], flow_ref.at[0, c, :, at(here)], own_sem.at[3 + c])
        own_flow.start()
        late = [own_flow]
        for k, peer in enumerate(sec_peers):
            copy = pltpu.make_async_remote_copy(
                src_ref=flows.at[peer, c],
                dst_ref=flow_ref.at[0, c, :, at(here)],
                send_sem=flow_send.at[c, k],
                recv_sem=flow_recv.at[c, k],
                device_id={"sec": peer},
                device_id_type=MESH,
            )
            copy.start()
            late.append(copy)
        outgoing += late

        if c == 0:
            take_cols(steps, soils)
        take_cols(c, head)
        prepare(slice(cols, ext_c))
        lax.fori_loop(1, total + 1, faces_across, 0)

        def first(s, acc):
            for j in range(layers):
                l = 1 + s * layers + j
                up, down = face_l[l - 1], face_l[l]
                fr, fc = face_r[l], face_c[l]
                v = head[l]
                whole = cap[l] + up + down + fr + shift(fr, 1, 0) + fc + shift(fc, 1, 1)
                flux_r = fr * (shift(v, -1, 0) - v)
                flux_c = fc * (shift(v, -1, 1) - v)
                res = up - down + up * (head[l - 1] - v) + down * (head[l + 1] - v)
                res = res + flux_r - shift(flux_r, 1, 0) + flux_c - shift(flux_c, 1, 1)
                if j == 0:
                    res = res + enter[s]
                if j == layers - 1:
                    res = res - leave[s]
                inverse = jnp.where(whole > 0.0, 1.0 / jnp.maximum(whole, 1e-30), 0.0)
                z = res * inverse
                diag[l] = whole
                dinv[l] = inverse
                t0[l] = z
                acc = acc + folded(res * z)
            return acc

        def land_copy(k, d, c=c):
            src = pl.ds(0, RIM) if d == 0 else pl.ds(rows - RIM, RIM)
            return pltpu.make_async_remote_copy(
                src_ref=basis[k].at[pl.ds(1, total), src, 0:cols],
                dst_ref=landed.at[c, k, d],
                send_sem=land_send.at[c, k, d],
                recv_sem=land_recv.at[c, k, d],
                device_id={"gx": lax.rem(gx + n_gx - 1, n_gx) if d == 0 else lax.rem(gx + 1, n_gx)},
                device_id_type=MESH,
            )

        def send_land(k):
            if c + 1 < steps:
                for d in (0, 1):
                    @pl.when(gx > 0 if d == 0 else gx < n_gx - 1)
                    def _(d=d):
                        land_copy(k, d).start()

        g = [lax.fori_loop(0, n_sec, first, none)]
        send_land(0)
        h = []
        for k in range(ITERS):
            def apply(l, acc, k=k):
                t = basis[k]
                fr, fc = face_r[l], face_c[l]
                v = t[l]
                near = face_l[l - 1] * t[l - 1] + face_l[l] * t[l + 1]
                near = near + fr * shift(v, -1, 0) + shift(fr * v, 1, 0)
                near = near + fc * shift(v, -1, 1) + shift(fc * v, 1, 1)
                ah = acc[0] + folded(v * near)
                ag = acc[1]
                if k + 1 < ITERS:
                    new = dinv[l] * near
                    if k > 0:
                        new = 2.0 * new - basis[k - 1][l]
                    basis[k + 1][l] = new
                    ag = ag + folded(diag[l] * new * new)
                return (ah, ag)

            ah, ag = lax.fori_loop(1, total + 1, apply, (none, none))
            h.append(ah)
            if k + 1 < ITERS:
                g.append(ag)
                send_land(k + 1)

        flat = jnp.concatenate([jnp.sum(v, axis=0, keepdims=True) for v in g + h], axis=0)
        part = LANES // (2 * ITERS)
        by = LANES // 2
        while by >= part:
            flat = flat + pltpu.roll(flat, by, 1)
            by //= 2
        which = lax.broadcasted_iota(jnp.int32, flat.shape, 0)
        group = lax.broadcasted_iota(jnp.int32, flat.shape, 1) // part
        mine = sec * n_gx + gx
        stats[c, mine] = jnp.sum(jnp.where(which == group, flat, 0.0), axis=0, keepdims=True)
        if c == 0:
            pl.semaphore_wait(met_sem, n_sec - 1)
        sends = []
        for k, peer in enumerate(everyone):
            copy = pltpu.make_async_remote_copy(
                src_ref=stats.at[c, mine],
                dst_ref=stats.at[c, mine],
                send_sem=sum_send.at[c, k],
                recv_sem=sum_recv.at[c, k],
                device_id=peer,
                device_id_type=MESH,
            )
            copy.start()
            sends.append(copy)
        for copy in sends:
            copy.wait()
        summed = stats[c, 0]
        for k in range(1, n_sec * n_gx):
            summed = summed + stats[c, k]
        parts = [
            jnp.sum(jnp.where(group[0:1] == k, summed, 0.0), axis=1, keepdims=True)
            for k in range(2 * ITERS)
        ]
        x = coefficients(parts[:ITERS], parts[ITERS:])
        x = [jnp.broadcast_to(v, (rows, cols)) for v in x]

        def update(l, carry):
            v = head[l, 0:rows, 0:cols]
            for k in range(ITERS):
                v = v + x[k] * basis[k][l, 0:rows, 0:cols]
            head[l, 0:rows, 0:cols] = v
            return carry

        if c + 1 == steps:
            for i in range(1, n_sec):
                peer = sec_peers[i - 1]
                lax.fori_loop(1 + peer * layers, 1 + (peer + 1) * layers, update, 0)
                back_copy(i - 1, peer).start()
                outgoing.append(back_copy(i - 1, peer))
            lax.fori_loop(1 + sec * layers, 1 + (sec + 1) * layers, update, 0)
        else:
            lax.fori_loop(1, total + 1, update, 0)
        if c + 1 < steps:
            for d in (0, 1):
                @pl.when(gx > 0 if d == 0 else gx < n_gx - 1)
                def _(d=d):
                    for k in range(ITERS):
                        land_copy(k, d).wait_send()

                @pl.when(gx < n_gx - 1 if d == 0 else gx > 0)
                def _(d=d):
                    for k in range(ITERS):
                        land_copy(k, d).wait_recv()

            def update_rim(l, carry):
                for d in (0, 1):
                    at_rows = slice(rows + d * RIM, rows + d * RIM + RIM)
                    v = head[l, at_rows, 0:cols]
                    for k in range(ITERS):
                        v = v + x[k][0:RIM] * landed[c, k, d, l - 1]
                    head[l, at_rows, 0:cols] = v
                return carry

            lax.fori_loop(1, total + 1, update_rim, 0)

    copy = pltpu.make_async_copy(head.at[layers_of(sec), 0:rows, 0:cols], out_ref.at[:, :, at(here)], own_sem.at[2])
    copy.start()
    outgoing.append(copy)
    for copy in outgoing:
        copy.wait()


def body(n_sec, n_gx, start, soil, conductivity, storage, rain):
    layers, rows, wide = start.shape
    steps = rain.shape[0]
    cols = wide // n_sec
    total = layers * n_sec
    assert total * RIM <= LANES and cols % LANES == 0 and rows % RIM == 0 and n_sec == 4
    ext = (rows + 2 * RIM, cols + LANES)
    f32 = jnp.float32
    field = pltpu.VMEM((total + 2,) + ext, f32)
    per_sec = pltpu.VMEM((n_sec,) + ext, f32)
    dma = pltpu.SemaphoreType.DMA
    vmem = pl.BlockSpec(memory_space=pltpu.VMEM)
    hbm = pl.BlockSpec(memory_space=pl.ANY)
    smem = pl.BlockSpec(memory_space=pltpu.SMEM)
    return tuple(pl.pallas_call(
        functools.partial(kernel, n_sec, n_gx, steps, conductivity.shape[0]),
        out_shape=(
            jax.ShapeDtypeStruct(start.shape, f32),
            jax.ShapeDtypeStruct((1, steps, rows, wide), f32),
        ),
        in_specs=[hbm, hbm, smem, smem, vmem],
        out_specs=(hbm, hbm),
        scratch_shapes=[field, pltpu.VMEM((total + 2,) + ext, jnp.int32)]
        + [field] * 13
        + [per_sec] * 3
        + [
            pltpu.VMEM((steps,) + ext, f32),
            pltpu.VMEM((n_sec, steps, rows, cols), f32),
            pltpu.VMEM((steps, 2, ext[0], LANES), f32),
            pltpu.VMEM((steps, 2, ext[0], LANES), f32),
            pltpu.VMEM((2, ext[0], LANES), jnp.int32),
            pltpu.VMEM((2, ext[0], LANES), jnp.int32),
            pltpu.VMEM((steps, ITERS, 2, total, RIM, cols), f32),
            pltpu.VMEM((steps, n_sec * n_gx, 1, LANES), f32),
            pltpu.SemaphoreType.REGULAR,
            dma((3 + steps,)),
            dma((2, n_sec - 1)),
            dma((2, n_sec - 1)),
            dma((steps + 1, 2)),
            dma((steps + 1, 2)),
            dma((3, 2)),
            dma((3, 2)),
            dma((steps, ITERS, 2)),
            dma((steps, ITERS, 2)),
            dma((steps, n_sec * n_gx)),
            dma((steps, n_sec * n_gx)),
            dma((steps, n_sec - 1)),
            dma((steps, n_sec - 1)),
            dma((n_sec - 1,)),
            dma((n_sec - 1,)),
        ],
        compiler_params=pltpu.CompilerParams(collective_id=0, has_side_effects=True),
    )(start, soil, conductivity, storage, rain))


def solution(mesh):
    placed = (P("sec", "gx", None), P("sec", "gx", None), P(), P(), P(None, "gx", None))
    return jax.shard_map(
        functools.partial(body, mesh.shape["sec"], mesh.shape["gx"]),
        mesh=mesh,
        in_specs=placed,
        out_specs=(P("sec", "gx", None), P("sec", None, "gx", None)),
        check_vma=False,
    )
```
